512 devices in a mesh: frame: 16 (over y, core), tok: 32 (over x, z).
Axes of the slice: x: 4, y: 8, z: 8, core: 2. Of those that a mesh axis runs over, the one named last changes fastest.
Arguments:
- inputs: bfloat16 [16, 24576, 512], P('frame', 'tok'), may hold values from -16 to 16
- kv_weight: bfloat16 [512, 2048], replicated, may hold values from -0.25 to 0.25
- latent_queries: bfloat16 [1024, 1024], P('tok'), may hold values from -21 to 21
- mix_gain: float32 [3072], replicated, may hold values from 0.5 to 2
- mix_weight: bfloat16 [3072, 1024], P(None, 'tok'), may hold values from -0.109375 to 0.109375
- output_queries: bfloat16 [16, 4096, 1024], P('frame', 'tok'), may hold values from -28 to 28
Outputs:
- decoded: float32 [16, 4096, 1024], P('frame', 'tok')
The draws below stay inside these ranges and needn't reach their ends.
All inputs are finite; a program needn't handle non-finite values.
Results may differ from the reference program's by a relative error of at most 0.035.
Values may be sent and summed in bfloat16 or wider, within the bound.
No kernel may reach another device: no remote copies, remote signals or barrier semaphores. Data moves between devices by JAX's collectives and lax.ppermute only.
A program may use at most 128 MiB of HBM per device.

```python
import math
import jax
import jax.numpy as jnp
from jax import lax

C = 512
D = 1024
LATENTS = 1024
HEADS = 8
HEAD_DIM = 128
IN_DEV = 768
FRAMES = 16
INPUTS = 24576
OUTPUTS = 4096
N_TOK = 32


def draw_inputs(key, part):
    key_base, key_frame = jax.random.split(key)
    ramp = 3.0 ** (jnp.arange(FRAMES, dtype=jnp.float32) / max(FRAMES - 1, 1))
    jitter = jax.random.uniform(key_frame, (FRAMES,), jnp.float32, 0.8, 1.25)
    base_draw = jnp.clip(jax.random.normal(key_base, (FRAMES, INPUTS, C), jnp.float32), -4.0, 4.0)
    return (base_draw * (ramp * jitter)[:, None, None]).astype(jnp.bfloat16)


def spread_queries(key, count):
    key_base = jax.random.fold_in(jax.random.fold_in(key, 7), 0)
    base_draw = jnp.clip(jax.random.normal(key_base, (count, D), jnp.float32), -4.0, 4.0)
    return base_draw.astype(jnp.bfloat16)


def draw_latent_queries(key, part):
    return spread_queries(key, LATENTS)


def draw_output_queries(key, part):
    frame_keys = jax.random.split(jax.random.fold_in(key, 11), FRAMES)
    return jax.vmap(lambda frame_key: spread_queries(frame_key, OUTPUTS))(frame_keys)


def levels(rng, shape, shards, least, high):
    factor_of = 1.0
    for dim, blocks in shards:
        steps = jax.random.uniform(jax.random.fold_in(jax.random.fold_in(rng, 6), dim), (blocks,), jnp.float32, least / len(shards), high / len(shards))
        factor_of = factor_of * jnp.repeat(jnp.exp(steps), shape[dim] // blocks).reshape((-1,) + (1,) * (len(shape) - 1 - dim))
    return factor_of


def centred(key, shape, deviation, reach, cuts=(), kind=jnp.bfloat16):
    level = levels(key, shape, cuts, -0.22, 0.18) if cuts else 1.0
    result = jax.random.normal(key, shape, jnp.float32) * deviation * level
    return jnp.minimum(jnp.maximum(result, -reach), reach).astype(kind)


def setup_inputs(seed: int = 0) -> dict:
    arg_keys = jax.random.split(jax.random.key(seed), 7)
    inputs = draw_inputs(jax.random.fold_in(arg_keys[6], 71), 0)
    kv_weight = centred(arg_keys[1], (C, 2 * D), C ** -0.5, 0.25)
    latent_queries = draw_latent_queries(jax.random.fold_in(arg_keys[6], 71), 0)
    mix_gain = jnp.clip(jnp.exp(jax.random.uniform(arg_keys[3], (3 * D,), jnp.float32, math.log(0.5), math.log(2.0))), 0.5, 2.0)
    mix_weight = centred(arg_keys[4], (3 * D, D), (3 * D) ** -0.5, 0.109375, ((1, 32),))
    output_queries = draw_output_queries(jax.random.fold_in(arg_keys[6], 71), 0)
    return {"inputs": inputs, "kv_weight": kv_weight, "latent_queries": latent_queries, "mix_gain": mix_gain, "mix_weight": mix_weight, "output_queries": output_queries}


def attend_heads(queries, keys, values):
    maxima = []
    numers = []
    denoms = []
    for head_index in range(HEADS):
        low_col = head_index * HEAD_DIM
        high_col = low_col + HEAD_DIM
        scores = lax.dot_general(queries[:, low_col:high_col], keys[:, low_col:high_col], (((1,), (1,)), ((), ())), preferred_element_type=jnp.float32) / math.sqrt(HEAD_DIM)
        row_peak = lax.optimization_barrier(jnp.max(scores, axis=1))
        weights = jnp.exp(scores - row_peak[:, None])
        denoms.append(lax.optimization_barrier(jnp.sum(weights, axis=1)))
        numers.append(jnp.dot(weights.astype(jnp.bfloat16), values[:, low_col:high_col], preferred_element_type=jnp.float32))
        maxima.append(row_peak)
    return (jnp.stack(maxima, axis=1), jnp.concatenate(numers, axis=1), jnp.stack(denoms, axis=1))

def decode_heads(queries, latent_rows):
    pieces = []
    for head_index in range(HEADS):
        low_col = head_index * HEAD_DIM
        high_col = low_col + HEAD_DIM
        scores = lax.dot_general(queries[:, low_col:high_col], latent_rows[:, low_col:high_col], (((1,), (1,)), ((), ())), preferred_element_type=jnp.float32) / math.sqrt(HEAD_DIM)
        row_peak = lax.optimization_barrier(jnp.max(scores, axis=1))
        weights = jnp.exp(scores - row_peak[:, None])
        denom_sum = lax.optimization_barrier(jnp.sum(weights, axis=1))
        summed = jnp.dot(weights.astype(jnp.bfloat16), latent_rows[:, low_col:high_col], preferred_element_type=jnp.float32)
        pieces.append(summed / denom_sum[:, None])
    return jnp.concatenate(pieces, axis=1)

def reference(inputs, kv_weight, latent_queries, mix_gain, mix_weight, output_queries):

    def encode_frame(frame_inputs):
        key_values = jnp.dot(frame_inputs, kv_weight, preferred_element_type=jnp.float32).astype(jnp.bfloat16)
        blocks = key_values.reshape(N_TOK, IN_DEV, 2 * D)

        def one_block(state_carry, block_rows):
            return (state_carry, attend_heads(latent_queries, block_rows[:, :D], block_rows[:, D:]))
        unused, parts = lax.scan(one_block, jnp.zeros((), jnp.float32), blocks)
        maxima, numers, denoms = parts
        peak_all = lax.optimization_barrier(jnp.max(maxima, axis=0))
        rescale = jnp.exp(maxima - peak_all[None])
        numer_terms = (numers.reshape(N_TOK, LATENTS, HEADS, HEAD_DIM) * rescale[:, :, :, None]).astype(jnp.bfloat16)
        denom_terms = (denoms * rescale).astype(jnp.bfloat16)
        numer_terms, denom_terms = lax.optimization_barrier((numer_terms, denom_terms))
        numerator = lax.optimization_barrier(jnp.sum(numer_terms.astype(jnp.float32), axis=0))
        denominator = lax.optimization_barrier(jnp.sum(denom_terms.astype(jnp.float32), axis=0))
        return (numerator / denominator[:, :, None]).reshape(LATENTS, D).astype(jnp.bfloat16)
    latents = lax.map(encode_frame, inputs)
    prior_one = jnp.concatenate([jnp.zeros((1, LATENTS, D), jnp.bfloat16), latents[:-1]], axis=0)
    prior_two = jnp.concatenate([jnp.zeros((2, LATENTS, D), jnp.bfloat16), latents[:-2]], axis=0)[:FRAMES]
    joined = jnp.concatenate([latents, prior_one, prior_two], axis=2).astype(jnp.float32)
    inverse = lax.rsqrt(lax.optimization_barrier(jnp.mean(joined * joined, axis=2)) + 1e-06)
    scaled = (joined * mix_gain).astype(jnp.bfloat16)
    product = jnp.dot(scaled.reshape(FRAMES * LATENTS, 3 * D), mix_weight, preferred_element_type=jnp.float32).reshape(FRAMES, LATENTS, D)
    mixed = jax.nn.gelu(product * inverse[:, :, None], approximate=False).astype(jnp.bfloat16)

    def decode_frame(frame_pair):
        return decode_heads(frame_pair[0], frame_pair[1])
    return lax.map(decode_frame, (output_queries, mixed))
```

```python
import math

import jax
import jax.numpy as jnp
from jax import lax
from jax.experimental import pallas as pl
from jax.experimental.pallas import tpu as pltpu
from jax.sharding import Mesh
from jax.sharding import PartitionSpec as P

HEADS = 8
HEAD_DIM = 128
EXP2_SCALE = math.log2(math.e) / math.sqrt(HEAD_DIM)
FRAME = ("y", "core")
EXTRA = 16
INTERPRET = False


def shift(block, axis, distance):
    size = lax.axis_size(axis)
    return lax.ppermute(block, axis, [(i, (i + distance) % size) for i in range(size)])


def from_behind(block, axis, distance):
    devices = range(lax.axis_size(axis))
    route = [(i - distance, i) for i in devices if i - distance in devices]
    return lax.ppermute(block, axis, route)


def gather(block, axis):
    copies = jnp.broadcast_to(block[None], (lax.axis_size(axis),) + block.shape)
    return lax.all_to_all(copies, axis, 0, 0, tiled=True)


def dot_nt(a, b):
    return lax.dot_general(a, b, (((1,), (1,)), ((), ())), preferred_element_type=jnp.float32)


def attend_body(q_ref, w_ref, *refs):
    in_refs, out_ref, kv_ref = refs[:-2], refs[-2], refs[-1]
    width = w_ref.shape[1]
    heads = width // (2 * HEAD_DIM)

    @pl.when(pl.program_id(0) == 0)
    def _():
        low = 0
        for in_ref in in_refs:
            rows = in_ref.shape[0]
            kv_ref[low : low + rows, :] = jnp.dot(
                in_ref[...], w_ref[...], preferred_element_type=jnp.float32
            ).astype(jnp.bfloat16)
            low += rows

    tile = q_ref.shape[0]
    blocks, _, _ = out_ref.shape
    rows = tile // blocks
    for h in range(heads):
        cols = slice(h * HEAD_DIM, (h + 1) * HEAD_DIM)
        scores = dot_nt(q_ref[:, cols], kv_ref[:, cols])
        peak = jnp.max(scores, axis=1, keepdims=True)
        weights = jnp.exp2((scores - peak) * EXP2_SCALE)
        den = jnp.sum(weights, axis=1, keepdims=True)
        value_cols = slice(width // 2 + h * HEAD_DIM, width // 2 + (h + 1) * HEAD_DIM)
        num = jnp.dot(
            weights.astype(jnp.bfloat16), kv_ref[:, value_cols], preferred_element_type=jnp.float32
        )
        first = peak.astype(jnp.bfloat16).astype(jnp.float32)
        second = (peak - first).astype(jnp.bfloat16).astype(jnp.float32)
        third = peak - first - second
        lane = lax.broadcasted_iota(jnp.int32, (tile, HEAD_DIM), 1)
        packed = jnp.where(
            lane == 0, first, jnp.where(lane == 1, second, jnp.where(lane == 2, third, den))
        )
        packed = packed.T
        for b in range(blocks):
            out_ref[b, :rows, cols] = num[b * rows : (b + 1) * rows].astype(jnp.bfloat16)
            out_ref[b, rows:, cols] = packed[:EXTRA, b * rows : (b + 1) * rows].astype(jnp.bfloat16)


def attend(queries, weight, inputs, blocks, tile):
    latents, width = queries.shape
    rows = latents // blocks
    per_step = tile // rows
    return pl.pallas_call(
        attend_body,
        grid=(latents // tile,),
        in_specs=[
            pl.BlockSpec((tile, width), lambda i: (i, 0)),
            pl.BlockSpec(weight.shape, lambda i: (0, 0)),
        ]
        + [pl.BlockSpec(block.shape, lambda i: (0, 0)) for block in inputs],
        out_specs=pl.BlockSpec((per_step, rows + EXTRA, width), lambda i: (i, 0, 0)),
        out_shape=jax.ShapeDtypeStruct((blocks, rows + EXTRA, width), jnp.bfloat16),
        scratch_shapes=[pltpu.VMEM((sum(b.shape[0] for b in inputs), 2 * width), jnp.bfloat16)],
        compiler_params=pltpu.CompilerParams(vmem_limit_bytes=48 * 1024 * 1024),
        interpret=INTERPRET,
        name="attend",
    )(queries, weight, *inputs)


def combine_body(part_ref, out_ref):
    blocks, height, width = part_ref.shape
    rows = height - EXTRA
    peaks = []
    dens = []
    for b in range(blocks):
        extra = part_ref[b, rows:, :].astype(jnp.float32)
        peaks.append(extra[0:1] + extra[1:2] + extra[2:3])
        dens.append(extra[3:4])
    top = peaks[0]
    for peak in peaks[1:]:
        top = jnp.maximum(top, peak)
    scales = [jnp.exp2((peak - top) * EXP2_SCALE) for peak in peaks]
    den = scales[0] * dens[0]
    for scale, part in zip(scales[1:], dens[1:]):
        den = den + scale * part
    pad = jnp.zeros((HEAD_DIM - blocks - 1, width), jnp.float32)
    table = jnp.concatenate(scales + [den, pad], axis=0)
    for h in range(width // HEAD_DIM):
        cols = slice(h * HEAD_DIM, (h + 1) * HEAD_DIM)
        turned = table[:, cols].T
        total = jnp.zeros((rows, HEAD_DIM), jnp.float32)
        for b in range(blocks):
            total = total + part_ref[b, :rows, cols].astype(jnp.float32) * turned[:, b : b + 1]
        out_ref[:, cols] = (total / turned[:, blocks : blocks + 1]).astype(jnp.bfloat16)


def combine(parts):
    blocks, height, width = parts.shape
    return pl.pallas_call(
        combine_body,
        out_shape=jax.ShapeDtypeStruct((height - EXTRA, width), jnp.bfloat16),
        interpret=INTERPRET,
        name="combine",
    )(parts)


def decode_body(q_ref, mixed_ref, out_ref):
    rows, width = q_ref.shape
    for h in range(width // HEAD_DIM):
        cols = slice(h * HEAD_DIM, (h + 1) * HEAD_DIM)
        scores = dot_nt(q_ref[:, cols], mixed_ref[:, cols])
        peak = jnp.max(scores, axis=1, keepdims=True)
        weights = jnp.exp2((scores - peak) * EXP2_SCALE)
        den = jnp.sum(weights, axis=1, keepdims=True)
        num = jnp.dot(
            weights.astype(jnp.bfloat16), mixed_ref[:, cols], preferred_element_type=jnp.float32
        )
        out_ref[:, cols] = num / den


def decode(queries, mixed, tile):
    count, width = queries.shape
    return pl.pallas_call(
        decode_body,
        grid=(count // tile,),
        in_specs=[
            pl.BlockSpec((tile, width), lambda i: (i, 0)),
            pl.BlockSpec(mixed.shape, lambda i: (0, 0)),
        ],
        out_specs=pl.BlockSpec((tile, width), lambda i: (i, 0)),
        out_shape=jax.ShapeDtypeStruct((count, width), jnp.float32),
        compiler_params=pltpu.CompilerParams(vmem_limit_bytes=48 * 1024 * 1024),
        interpret=INTERPRET,
        name="decode",
    )(queries, mixed)


def local(inputs, kv_weight, latent_queries, mix_gain, mix_weight, output_queries):
    groups = lax.axis_size("x")
    members = lax.axis_size("z")
    place = lax.axis_index("x")
    latent_width = HEADS * HEAD_DIM
    width = latent_width // groups

    mine = inputs[0]
    half = mine.shape[0] // 2
    above = shift(mine, "x", -1)
    below = shift(mine, "x", 1)
    far_low = shift(above[:half], "x", -1)
    far_high = shift(below[half:], "x", 1)

    mix_t = lax.all_gather(mix_weight.T, "z", axis=0, tiled=True)

    own_queries = jnp.concatenate([latent_queries, output_queries[0]], axis=0)
    count = own_queries.shape[0]
    rows = latent_queries.shape[0]
    split = jnp.stack(
        [own_queries[:, g * width : (g + 1) * width] for g in range(groups)], axis=0
    )
    split = lax.all_to_all(split, "x", 0, 0, tiled=True)
    queries = gather(split[:, :rows].reshape(groups * rows, width), "z")
    queries = queries.reshape(members * groups * rows, width)
    frame_queries = split[:, rows:].reshape(groups * (count - rows), width)

    weight = jnp.concatenate(
        [
            lax.dynamic_slice_in_dim(kv_weight, place * width, width, axis=1),
            lax.dynamic_slice_in_dim(kv_weight, latent_width + place * width, width, axis=1),
        ],
        axis=1,
    )
    parts = attend(
        queries, weight, (mine, above, below, far_low, far_high), members, queries.shape[0] // 4
    )
    parts = lax.all_to_all(parts, "z", 0, 0, tiled=True)
    latents = combine(parts)

    prior_one = from_behind(latents, FRAME, 1)
    prior_two = from_behind(latents, FRAME, 2)
    window = gather(jnp.stack([latents, prior_one, prior_two], axis=0), "x")
    joined = jnp.concatenate([window[g, t] for t in range(3) for g in range(groups)], axis=1)
    joined_f32 = joined.astype(jnp.float32)
    squares = jnp.sum(joined_f32 * joined_f32, axis=1, keepdims=True)
    scaled = (joined_f32 * mix_gain).astype(jnp.bfloat16)
    inverse = lax.rsqrt(squares / (3 * latent_width) + 1e-06)
    summed = dot_nt(scaled, mix_t)
    mixed = jax.nn.gelu(summed * inverse, approximate=False).astype(jnp.bfloat16)
    mixed = gather(mixed, "z")
    mixed = mixed.reshape(members * mixed.shape[1], width)

    decoded = decode(frame_queries, mixed, frame_queries.shape[0] // 2)
    decoded = decoded.reshape(groups, count - rows, width)
    decoded = lax.all_to_all(decoded, "x", 0, 0, tiled=True)
    return jnp.concatenate([decoded[g] for g in range(groups)], axis=1)[None]


def solution(mesh):
    grid = Mesh(mesh.devices.reshape(8, 2, 4, 8), ("y", "core", "x", "z"))
    tok = ("x", "z")
    return jax.shard_map(
        local,
        mesh=grid,
        in_specs=(P(FRAME, tok, None), P(), P(tok, None), P(), P(None, tok), P(FRAME, tok, None)),
        out_specs=P(FRAME, tok, None),
        check_vma=False,
    )
```

```python
import math

import jax
import jax.numpy as jnp
from jax import lax
from jax.experimental import pallas as pl
from jax.experimental.pallas import tpu as pltpu
from jax.sharding import Mesh
from jax.sharding import PartitionSpec as P


HEADS = 8
HEAD_DIM = 128
EXP2_SCALE = math.log2(math.e) / math.sqrt(HEAD_DIM)
FRAME = ("y", "core")
EXTRA = 16
TAIL = 8
VMEM_BYTES = 32 * 1024 * 1024
INTERPRET = False


def shift(block, axis, distance):
    size = lax.axis_size(axis)
    return lax.ppermute(block, axis, [(i, (i + distance) % size) for i in range(size)])


def from_behind(block, axis, distance):
    devices = range(lax.axis_size(axis))
    route = [(i - distance, i) for i in devices if i - distance in devices]
    return lax.ppermute(block, axis, route)


def gather(block, axis):
    copies = jnp.broadcast_to(block[None], (lax.axis_size(axis),) + block.shape)
    return lax.all_to_all(copies, axis, 0, 0, tiled=True)


def partner(block):
    return lax.ppermute(block, "core", [(0, 1), (1, 0)])


def dot_nt(a, b):
    return lax.dot_general(a, b, (((1,), (1,)), ((), ())), preferred_element_type=jnp.float32)


def head_cols(h):
    return slice(h * HEAD_DIM, (h + 1) * HEAD_DIM)


def project_inputs(in_refs, w_ref, kv_ref):
    low = 0
    for in_ref in in_refs:
        rows = in_ref.shape[0]
        kv_ref[low : low + rows, :] = jnp.dot(
            in_ref[...], w_ref[...], preferred_element_type=jnp.float32
        ).astype(jnp.bfloat16)
        low += rows


def pick_queries(core_ref, mine_ref, other_ref, tile_ref):
    step = pl.program_id(0)
    tile = tile_ref.shape[0]
    per_half = mine_ref.shape[0] // tile
    start = pl.multiple_of((step % per_half) * tile, tile)
    is_mine = step // per_half == core_ref[0]

    @pl.when(is_mine)
    def _():
        tile_ref[...] = mine_ref[pl.ds(start, tile), :]

    @pl.when(jnp.logical_not(is_mine))
    def _():
        tile_ref[...] = other_ref[pl.ds(start, tile), :]


def lanes(values, shape):
    lane = lax.broadcasted_iota(jnp.int32, shape, 1)
    result = jnp.broadcast_to(values[-1], shape)
    for k in range(len(values) - 2, -1, -1):
        result = jnp.where(lane == k, values[k], result)
    return result


def near_body(core_ref, mine_ref, other_ref, w_ref, *refs):
    in_refs, (num_ref, stat_ref, kv_ref, q_ref) = refs[:-4], refs[-4:]
    width = mine_ref.shape[1]

    @pl.when(pl.program_id(0) == 0)
    def _():
        project_inputs(in_refs, w_ref, kv_ref)

    pick_queries(core_ref, mine_ref, other_ref, q_ref)
    tile = q_ref.shape[0]
    for h in range(width // HEAD_DIM):
        cols = head_cols(h)
        scores = dot_nt(q_ref[:, cols], kv_ref[:, cols])
        peak = jnp.max(scores, axis=1, keepdims=True)
        weights = jnp.exp2((scores - peak) * EXP2_SCALE)
        den = jnp.sum(weights, axis=1, keepdims=True)
        value_cols = slice(width + h * HEAD_DIM, width + (h + 1) * HEAD_DIM)
        num_ref[:, cols] = jnp.dot(
            weights.astype(jnp.bfloat16), kv_ref[:, value_cols], preferred_element_type=jnp.float32
        )
        stat_ref[:, cols] = lanes([peak, den], (tile, HEAD_DIM))


def far_body(core_ref, mine_ref, other_ref, w_ref, num_ref, stat_ref, *refs):
    in_refs, (out_ref, kv_ref, q_ref) = refs[:-3], refs[-3:]
    width = mine_ref.shape[1]

    @pl.when(pl.program_id(0) == 0)
    def _():
        project_inputs(in_refs, w_ref, kv_ref)

    pick_queries(core_ref, mine_ref, other_ref, q_ref)
    tile = q_ref.shape[0]
    blocks = out_ref.shape[0]
    rows = tile // blocks
    for h in range(width // HEAD_DIM):
        cols = head_cols(h)
        near_peak = stat_ref[:, h * HEAD_DIM : h * HEAD_DIM + 1]
        near_den = stat_ref[:, h * HEAD_DIM + 1 : h * HEAD_DIM + 2]
        scores = dot_nt(q_ref[:, cols], kv_ref[:, cols])
        peak = jnp.maximum(jnp.max(scores, axis=1, keepdims=True), near_peak)
        weights = jnp.exp2((scores - peak) * EXP2_SCALE)
        rescale = jnp.exp2((near_peak - peak) * EXP2_SCALE)
        den = jnp.sum(weights, axis=1, keepdims=True) + rescale * near_den
        value_cols = slice(width + h * HEAD_DIM, width + (h + 1) * HEAD_DIM)
        num = rescale * num_ref[:, cols] + jnp.dot(
            weights.astype(jnp.bfloat16), kv_ref[:, value_cols], preferred_element_type=jnp.float32
        )
        first = peak.astype(jnp.bfloat16).astype(jnp.float32)
        second = (peak - first).astype(jnp.bfloat16).astype(jnp.float32)
        packed = lanes([first, second, peak - first - second, den], (tile, HEAD_DIM)).T
        for b in range(blocks):
            span = slice(b * rows, (b + 1) * rows)
            out_ref[b, :rows, cols] = num[span].astype(jnp.bfloat16)
            out_ref[b, rows:, cols] = packed[:EXTRA, span].astype(jnp.bfloat16)


def attend(core, mine, other, weight, near, far, blocks, tile):
    half, width = mine.shape
    latents = 2 * half
    rows = latents // blocks
    scalar = pl.BlockSpec(memory_space=pltpu.SMEM)

    def whole(block):
        return pl.BlockSpec(block.shape, lambda i: (0, 0))

    tiled = pl.BlockSpec((tile, width), lambda i: (i, 0))
    params = pltpu.CompilerParams(vmem_limit_bytes=VMEM_BYTES)
    common = (core, mine, other, weight)
    common_specs = [scalar, whole(mine), whole(other), whole(weight)]
    num, stat = pl.pallas_call(
        near_body,
        grid=(latents // tile,),
        in_specs=common_specs + [whole(block) for block in near],
        out_specs=(tiled, tiled),
        out_shape=(jax.ShapeDtypeStruct((latents, width), jnp.float32),) * 2,
        scratch_shapes=[
            pltpu.VMEM((sum(b.shape[0] for b in near), 2 * width), jnp.bfloat16),
            pltpu.VMEM((tile, width), jnp.bfloat16),
        ],
        compiler_params=params,
        interpret=INTERPRET,
        name="attend_near",
    )(*common, *near)
    return pl.pallas_call(
        far_body,
        grid=(latents // tile,),
        in_specs=common_specs + [tiled, tiled] + [whole(block) for block in far],
        out_specs=pl.BlockSpec((tile // rows, rows + EXTRA, width), lambda i: (i, 0, 0)),
        out_shape=jax.ShapeDtypeStruct((blocks, rows + EXTRA, width), jnp.bfloat16),
        scratch_shapes=[
            pltpu.VMEM((sum(b.shape[0] for b in far), 2 * width), jnp.bfloat16),
            pltpu.VMEM((tile, width), jnp.bfloat16),
        ],
        compiler_params=params,
        interpret=INTERPRET,
        name="attend_far",
    )(*common, num, stat, *far)


def combine_body(part_ref, query_ref, out_ref):
    blocks, height, width = part_ref.shape
    rows = height - EXTRA
    groups = out_ref.shape[0]
    peaks = []
    dens = []
    for b in range(blocks):
        extra = part_ref[b, rows:, :].astype(jnp.float32)
        peaks.append(extra[0:1] + extra[1:2] + extra[2:3])
        dens.append(extra[3:4])
    top = peaks[0]
    for peak in peaks[1:]:
        top = jnp.maximum(top, peak)
    scales = [jnp.exp2((peak - top) * EXP2_SCALE) for peak in peaks]
    den = scales[0] * dens[0]
    for scale, part in zip(scales[1:], dens[1:]):
        den = den + scale * part
    pad = jnp.zeros((HEAD_DIM - blocks - 1, width), jnp.float32)
    table = jnp.concatenate(scales + [den, pad], axis=0)
    for h in range(width // HEAD_DIM):
        cols = head_cols(h)
        turned = table[:, cols].T
        total = jnp.zeros((rows, HEAD_DIM), jnp.float32)
        for b in range(blocks):
            total = total + part_ref[b, :rows, cols].astype(jnp.float32) * turned[:, b : b + 1]
        latents = (total / turned[:, blocks : blocks + 1]).astype(jnp.bfloat16)
        for g in range(groups):
            out_ref[g, :rows, cols] = latents
    for g in range(groups):
        out_ref[g, rows:, :] = query_ref[:, g * width : (g + 1) * width]


def whole_spec(block):
    return pl.BlockSpec(block.shape, lambda i: (0,) * len(block.shape))


def combine(parts, queries, groups):
    _, height, width = parts.shape
    rows = height - EXTRA
    return pl.pallas_call(
        combine_body,
        grid=(1,),
        in_specs=[whole_spec(parts), whole_spec(queries)],
        out_specs=pl.BlockSpec((groups, rows + queries.shape[0], width), lambda i: (0, 0, 0)),
        out_shape=jax.ShapeDtypeStruct((groups, rows + queries.shape[0], width), jnp.bfloat16),
        compiler_params=pltpu.CompilerParams(vmem_limit_bytes=VMEM_BYTES // 2),
        interpret=INTERPRET,
        name="combine",
    )(parts, queries)


def turn(column):
    return jnp.broadcast_to(column, (column.shape[0], HEAD_DIM)).T


def products_body(core_ref, rows_ref, gain_ref, mine_ref, other_ref, own_ref, one_ref, two_ref):
    groups, _, width = rows_ref.shape
    full = groups * width
    half = mine_ref.shape[1]
    count = own_ref.shape[0] - TAIL
    squares = jnp.zeros((count, 1), jnp.float32)
    for g in range(groups):
        block = rows_ref[g, :count].astype(jnp.float32)
        squares = squares + jnp.sum(block * block, axis=1, keepdims=True)
    tail = turn(squares)[:TAIL]
    outs = (own_ref, one_ref, two_ref)
    for out_ref in outs:
        for h in range(width // HEAD_DIM):
            out_ref[count:, head_cols(h)] = tail

    def multiply(halves):
        for t, out_ref in enumerate(outs):
            total = jnp.zeros((count, width), jnp.float32)
            for g in range(groups):
                low = t * full + g * width
                block = rows_ref[g, :count].astype(jnp.float32) * gain_ref[:, low : low + width]
                part_ref = halves[low // half]
                at = low % half
                total = total + dot_nt(block.astype(jnp.bfloat16), part_ref[:, at : at + width])
            out_ref[:count, :] = total

    @pl.when(core_ref[0] == 0)
    def _():
        multiply((mine_ref, other_ref))

    @pl.when(core_ref[0] != 0)
    def _():
        multiply((other_ref, mine_ref))


def products(core, window, count, gain, mine, other):
    groups, _, width = window.shape
    return pl.pallas_call(
        products_body,
        grid=(1,),
        in_specs=[
            pl.BlockSpec(memory_space=pltpu.SMEM),
            pl.BlockSpec((groups, count, width), lambda i: (0, 0, 0)),
            pl.BlockSpec(gain.shape, lambda i: (0, 0)),
            pl.BlockSpec(mine.shape, lambda i: (0, 0)),
            pl.BlockSpec(other.shape, lambda i: (0, 0)),
        ],
        out_specs=(pl.BlockSpec((count + TAIL, width), lambda i: (0, 0)),) * 3,
        out_shape=(jax.ShapeDtypeStruct((count + TAIL, width), jnp.float32),) * 3,
        compiler_params=pltpu.CompilerParams(vmem_limit_bytes=VMEM_BYTES),
        interpret=INTERPRET,
        name="products",
    )(core, window, gain, mine, other)


def finish_body(own_ref, one_ref, two_ref, out_ref, *, features):
    members, count, width = out_ref.shape
    squares = own_ref[count:, :] + one_ref[count:, :] + two_ref[count:, :]
    inverse = lax.rsqrt(squares / features + 1e-06)
    for h in range(width // HEAD_DIM):
        cols = head_cols(h)
        pad = jnp.zeros((HEAD_DIM - TAIL, HEAD_DIM), jnp.float32)
        column = jnp.concatenate([inverse[:, cols], pad], axis=0).T[:, :1]
        product = own_ref[:count, cols] + one_ref[:count, cols] + two_ref[:count, cols]
        value = product * column
        mixed = (0.5 * value * (1.0 + lax.erf(value * math.sqrt(0.5)))).astype(jnp.bfloat16)
        for m in range(members):
            out_ref[m, :, cols] = mixed


def finish(own, one, two, members, features):
    height, width = own.shape
    return pl.pallas_call(
        lambda *refs: finish_body(*refs, features=features),
        grid=(1,),
        in_specs=[whole_spec(own), whole_spec(one), whole_spec(two)],
        out_specs=pl.BlockSpec((members, height - TAIL, width), lambda i: (0, 0, 0)),
        out_shape=jax.ShapeDtypeStruct((members, height - TAIL, width), jnp.bfloat16),
        compiler_params=pltpu.CompilerParams(vmem_limit_bytes=VMEM_BYTES // 2),
        interpret=INTERPRET,
        name="finish",
    )(own, one, two)


def decode_body(q_ref, mixed_ref, out_ref):
    groups, _, width = q_ref.shape
    for g in range(groups):
        for h in range(width // HEAD_DIM):
            cols = head_cols(h)
            scores = dot_nt(q_ref[g, :, cols], mixed_ref[:, cols])
            peak = jnp.max(scores, axis=1, keepdims=True)
            weights = jnp.exp2((scores - peak) * EXP2_SCALE)
            den = jnp.sum(weights, axis=1, keepdims=True)
            num = jnp.dot(
                weights.astype(jnp.bfloat16), mixed_ref[:, cols], preferred_element_type=jnp.float32
            )
            out_ref[g, :, cols] = num / den


def decode(window, count, mixed):
    groups, height, width = window.shape
    rows = height - count
    step = 2
    return pl.pallas_call(
        decode_body,
        grid=(groups // step,),
        in_specs=[
            pl.BlockSpec((step, rows, width), lambda i: (i, 1, 0)),
            pl.BlockSpec(mixed.shape, lambda i: (0, 0)),
        ],
        out_specs=pl.BlockSpec((step, rows, width), lambda i: (i, 0, 0)),
        out_shape=jax.ShapeDtypeStruct((groups, rows, width), jnp.float32),
        compiler_params=pltpu.CompilerParams(vmem_limit_bytes=VMEM_BYTES),
        interpret=INTERPRET,
        name="decode",
    )(window, mixed)


def local(inputs, kv_weight, latent_queries, mix_gain, mix_weight, output_queries):
    groups = lax.axis_size("x")
    members = lax.axis_size("z")
    place = lax.axis_index("x")
    core_index = lax.axis_index("core")
    core = core_index.reshape(1).astype(jnp.int32)
    latent_width = HEADS * HEAD_DIM
    width = latent_width // groups

    mine = inputs[0]
    half = mine.shape[0] // 2
    above = shift(mine, "x", -1)
    below = shift(mine, "x", 1)

    mix_t = mix_weight.T
    mix_half = mix_t.shape[1] // 2
    mix_mine = lax.dynamic_slice_in_dim(mix_t, core_index * mix_half, mix_half, axis=1)
    mix_mine = gather(mix_mine, "z").reshape(members * mix_t.shape[0], mix_half)
    mix_other = partner(mix_mine)

    rows = latent_queries.shape[0] // 2
    asked = lax.dynamic_slice_in_dim(latent_queries, core_index * rows, rows, axis=0)
    asked = jnp.stack([asked[:, g * width : (g + 1) * width] for g in range(groups)], axis=0)
    asked = jnp.broadcast_to(asked[:, None], (groups, members, rows, width))
    asked = asked.reshape(groups * members, rows, width)
    asked = lax.all_to_all(asked, ("x", "z"), 0, 0, tiled=True)
    asked = asked.reshape(groups * members * rows, width)
    asked_other = partner(asked)

    far_low = shift(above[:half], "x", -1)
    far_high = shift(below[half:], "x", 1)
    weight = jnp.concatenate(
        [
            lax.dynamic_slice_in_dim(kv_weight, place * width, width, axis=1),
            lax.dynamic_slice_in_dim(kv_weight, latent_width + place * width, width, axis=1),
        ],
        axis=1,
    )
    latents = groups * members * rows * 2
    parts = attend(
        core,
        asked,
        asked_other,
        weight,
        (mine, above, below),
        (far_low, far_high),
        members,
        latents // 4,
    )
    parts = lax.all_to_all(parts, "z", 0, 0, tiled=True)
    count = latents // members
    window = lax.all_to_all(combine(parts, output_queries[0], groups), "x", 0, 0, tiled=True)
    own, one, two = products(core, window, count, mix_gain[None], mix_mine, mix_other)
    one = from_behind(one, FRAME, 1)
    two = from_behind(two, FRAME, 2)
    mixed = finish(own, one, two, members, 3 * latent_width)
    mixed = lax.all_to_all(mixed, "z", 0, 0, tiled=True).reshape(latents, width)

    decoded = decode(window, count, mixed)
    decoded = lax.all_to_all(decoded, "x", 0, 0, tiled=True)
    return jnp.concatenate([decoded[g] for g in range(groups)], axis=1)[None]


def solution(mesh):
    grid = Mesh(mesh.devices.reshape(8, 2, 4, 8), ("y", "core", "x", "z"))
    tok = ("x", "z")
    return jax.shard_map(
        local,
        mesh=grid,
        in_specs=(P(FRAME, tok, None), P(), P(tok, None), P(), P(None, tok), P(FRAME, tok, None)),
        out_specs=P(FRAME, tok, None),
        check_vma=False,
    )
```

```python
import math

import jax
import jax.numpy as jnp
from jax import lax
from jax.experimental import pallas as pl
from jax.experimental.pallas import tpu as pltpu
from jax.sharding import Mesh
from jax.sharding import PartitionSpec as P


HEADS = 8
HEAD_DIM = 128
EXP2_SCALE = math.log2(math.e) / math.sqrt(HEAD_DIM)
FRAME = ("y", "core")
EXTRA = 16
TAIL = 8
XORS = (4, 2, 1)
MASKS = (0, 4, 2, 6, 1, 5, 3, 7)
VMEM_BYTES = 32 * 1024 * 1024
INTERPRET = False


def shift(block, axis, distance):
    size = lax.axis_size(axis)
    return lax.ppermute(block, axis, [(i, (i + distance) % size) for i in range(size)])


def from_behind(block, axis, distance):
    devices = range(lax.axis_size(axis))
    route = [(i - distance, i) for i in devices if i - distance in devices]
    return lax.ppermute(block, axis, route)


def across(block, axis, mask):
    return lax.ppermute(block, axis, [(i, i ^ mask) for i in range(lax.axis_size(axis))])


def partner(block):
    return lax.ppermute(block, "core", [(0, 1), (1, 0)])


def dot_nt(a, b):
    return lax.dot_general(a, b, (((1,), (1,)), ((), ())), preferred_element_type=jnp.float32)


def whole_spec(block):
    return pl.BlockSpec(block.shape, lambda i: (0,) * len(block.shape))


def head_cols(h):
    return slice(h * HEAD_DIM, (h + 1) * HEAD_DIM)


def project_inputs(in_refs, w_ref, kv_ref):
    low = 0
    for in_ref in in_refs:
        rows = in_ref.shape[0]
        kv_ref[low : low + rows, :] = jnp.dot(
            in_ref[...], w_ref[...], preferred_element_type=jnp.float32
        ).astype(jnp.bfloat16)
        low += rows


def pick_queries(core_ref, mine_ref, other_ref, tile_ref):
    step = pl.program_id(0)
    tile = tile_ref.shape[0]
    per_half = mine_ref.shape[0] // tile
    start = pl.multiple_of((step % per_half) * tile, tile)
    is_mine = step // per_half == core_ref[0]

    @pl.when(is_mine)
    def _():
        tile_ref[...] = mine_ref[pl.ds(start, tile), :]

    @pl.when(jnp.logical_not(is_mine))
    def _():
        tile_ref[...] = other_ref[pl.ds(start, tile), :]


def lanes(values, shape):
    lane = lax.broadcasted_iota(jnp.int32, shape, 1)
    result = jnp.broadcast_to(values[-1], shape)
    for k in range(len(values) - 2, -1, -1):
        result = jnp.where(lane == k, values[k], result)
    return result


def attend_body(core_ref, mine_ref, other_ref, w_ref, *refs):
    in_refs, (out_ref, kv_ref, q_ref) = refs[:-3], refs[-3:]
    width = mine_ref.shape[1]

    @pl.when(pl.program_id(0) == 0)
    def _():
        project_inputs(in_refs, w_ref, kv_ref)

    pick_queries(core_ref, mine_ref, other_ref, q_ref)
    tile = q_ref.shape[0]
    blocks = out_ref.shape[0]
    rows = tile // blocks
    for h in range(width // HEAD_DIM):
        cols = head_cols(h)
        scores = dot_nt(q_ref[:, cols], kv_ref[:, cols])
        peak = jnp.max(scores, axis=1, keepdims=True)
        weights = jnp.exp2((scores - peak) * EXP2_SCALE)
        den = jnp.sum(weights, axis=1, keepdims=True)
        value_cols = slice(width + h * HEAD_DIM, width + (h + 1) * HEAD_DIM)
        num = jnp.dot(
            weights.astype(jnp.bfloat16), kv_ref[:, value_cols], preferred_element_type=jnp.float32
        )
        first = peak.astype(jnp.bfloat16).astype(jnp.float32)
        second = (peak - first).astype(jnp.bfloat16).astype(jnp.float32)
        packed = lanes([first, second, peak - first - second, den], (tile, HEAD_DIM)).T
        for b in range(blocks):
            span = slice(b * rows, (b + 1) * rows)
            out_ref[b, :rows, cols] = num[span].astype(jnp.bfloat16)
            out_ref[b, rows:, cols] = packed[:EXTRA, span].astype(jnp.bfloat16)


def attend(core, mine, other, weight, inputs, blocks, tile):
    half, width = mine.shape
    latents = 2 * half
    rows = latents // blocks
    return pl.pallas_call(
        attend_body,
        grid=(latents // tile,),
        in_specs=[pl.BlockSpec(memory_space=pltpu.SMEM)]
        + [whole_spec(block) for block in (mine, other, weight) + inputs],
        out_specs=pl.BlockSpec((tile // rows, rows + EXTRA, width), lambda i: (i, 0, 0)),
        out_shape=jax.ShapeDtypeStruct((blocks, rows + EXTRA, width), jnp.bfloat16),
        scratch_shapes=[
            pltpu.VMEM((sum(b.shape[0] for b in inputs), 2 * width), jnp.bfloat16),
            pltpu.VMEM((tile, width), jnp.bfloat16),
        ],
        compiler_params=pltpu.CompilerParams(vmem_limit_bytes=VMEM_BYTES),
        interpret=INTERPRET,
        name="attend",
    )(core, mine, other, weight, *inputs)


def order_body(place_ref, first_ref, second_ref, out_ref):
    rows = out_ref.shape[0] // len(MASKS)
    half = len(MASKS) // 2
    for j, mask in enumerate(MASKS):
        part_ref = (first_ref, second_ref)[j // half]
        low = (j % half) * rows
        at = pl.multiple_of((place_ref[0] ^ mask) * rows, rows)
        out_ref[pl.ds(at, rows), :] = part_ref[low : low + rows, :]


def order(place, first, second):
    shape = (2 * first.shape[0], first.shape[1])
    return pl.pallas_call(
        order_body,
        grid=(1,),
        in_specs=[pl.BlockSpec(memory_space=pltpu.SMEM), whole_spec(first), whole_spec(second)],
        out_specs=pl.BlockSpec(shape, lambda i: (0, 0)),
        out_shape=jax.ShapeDtypeStruct(shape, first.dtype),
        compiler_params=pltpu.CompilerParams(vmem_limit_bytes=VMEM_BYTES // 2),
        interpret=INTERPRET,
        name="order",
    )(place, first, second)


def combine_body(part_ref, out_ref):
    blocks, height, width = part_ref.shape
    rows = height - EXTRA
    groups = out_ref.shape[0]
    peaks = []
    dens = []
    for b in range(blocks):
        extra = part_ref[b, rows:, :].astype(jnp.float32)
        peaks.append(extra[0:1] + extra[1:2] + extra[2:3])
        dens.append(extra[3:4])
    top = peaks[0]
    for peak in peaks[1:]:
        top = jnp.maximum(top, peak)
    scales = [jnp.exp2((peak - top) * EXP2_SCALE) for peak in peaks]
    den = scales[0] * dens[0]
    for scale, part in zip(scales[1:], dens[1:]):
        den = den + scale * part
    pad = jnp.zeros((HEAD_DIM - blocks - 1, width), jnp.float32)
    table = jnp.concatenate(scales + [den, pad], axis=0)
    for h in range(width // HEAD_DIM):
        cols = head_cols(h)
        turned = table[:, cols].T
        total = jnp.zeros((rows, HEAD_DIM), jnp.float32)
        for b in range(blocks):
            total = total + part_ref[b, :rows, cols].astype(jnp.float32) * turned[:, b : b + 1]
        latents = (total / turned[:, blocks : blocks + 1]).astype(jnp.bfloat16)
        for g in range(groups):
            out_ref[g, :, cols] = latents


def combine(parts, groups):
    _, height, width = parts.shape
    rows = height - EXTRA
    return pl.pallas_call(
        combine_body,
        grid=(1,),
        in_specs=[whole_spec(parts)],
        out_specs=pl.BlockSpec((groups, rows, width), lambda i: (0, 0, 0)),
        out_shape=jax.ShapeDtypeStruct((groups, rows, width), jnp.bfloat16),
        compiler_params=pltpu.CompilerParams(vmem_limit_bytes=VMEM_BYTES // 2),
        interpret=INTERPRET,
        name="combine",
    )(parts)


def turn(column):
    return jnp.broadcast_to(column, (column.shape[0], HEAD_DIM)).T


def products_body(core_ref, rows_ref, gain_ref, mine_ref, other_ref, own_ref, one_ref, two_ref):
    groups, _, width = rows_ref.shape
    full = groups * width
    half = mine_ref.shape[1]
    count = own_ref.shape[0] - TAIL
    squares = jnp.zeros((count, 1), jnp.float32)
    for g in range(groups):
        block = rows_ref[g].astype(jnp.float32)
        squares = squares + jnp.sum(block * block, axis=1, keepdims=True)
    tail = turn(squares)[:TAIL]
    outs = (own_ref, one_ref, two_ref)
    for out_ref in outs:
        for h in range(width // HEAD_DIM):
            out_ref[count:, head_cols(h)] = tail

    def multiply(halves):
        for t, out_ref in enumerate(outs):
            total = jnp.zeros((count, width), jnp.float32)
            for g in range(groups):
                low = t * full + g * width
                block = rows_ref[g].astype(jnp.float32) * gain_ref[:, low : low + width]
                part_ref = halves[low // half]
                at = low % half
                total = total + dot_nt(block.astype(jnp.bfloat16), part_ref[:, at : at + width])
            out_ref[:count, :] = total

    @pl.when(core_ref[0] == 0)
    def _():
        multiply((mine_ref, other_ref))

    @pl.when(core_ref[0] != 0)
    def _():
        multiply((other_ref, mine_ref))


def products(core, window, gain, mine, other):
    _, count, width = window.shape
    return pl.pallas_call(
        products_body,
        grid=(1,),
        in_specs=[
            pl.BlockSpec(memory_space=pltpu.SMEM),
        ]
        + [whole_spec(block) for block in (window, gain, mine, other)],
        out_specs=(pl.BlockSpec((count + TAIL, width), lambda i: (0, 0)),) * 3,
        out_shape=(jax.ShapeDtypeStruct((count + TAIL, width), jnp.float32),) * 3,
        compiler_params=pltpu.CompilerParams(vmem_limit_bytes=VMEM_BYTES),
        interpret=INTERPRET,
        name="products",
    )(core, window, gain, mine, other)


def finish_body(own_ref, one_ref, two_ref, out_ref, *, features):
    members, count, width = out_ref.shape
    squares = own_ref[count:, :] + one_ref[count:, :] + two_ref[count:, :]
    inverse = lax.rsqrt(squares / features + 1e-06)
    for h in range(width // HEAD_DIM):
        cols = head_cols(h)
        pad = jnp.zeros((HEAD_DIM - TAIL, HEAD_DIM), jnp.float32)
        column = jnp.concatenate([inverse[:, cols], pad], axis=0).T[:, :1]
        product = own_ref[:count, cols] + one_ref[:count, cols] + two_ref[:count, cols]
        value = product * column
        mixed = (0.5 * value * (1.0 + lax.erf(value * math.sqrt(0.5)))).astype(jnp.bfloat16)
        for m in range(members):
            out_ref[m, :, cols] = mixed


def finish(own, one, two, members, features):
    height, width = own.shape
    return pl.pallas_call(
        lambda *refs: finish_body(*refs, features=features),
        grid=(1,),
        in_specs=[whole_spec(own), whole_spec(one), whole_spec(two)],
        out_specs=pl.BlockSpec((members, height - TAIL, width), lambda i: (0, 0, 0)),
        out_shape=jax.ShapeDtypeStruct((members, height - TAIL, width), jnp.bfloat16),
        compiler_params=pltpu.CompilerParams(vmem_limit_bytes=VMEM_BYTES // 2),
        interpret=INTERPRET,
        name="finish",
    )(own, one, two)


def decode_body(place_ref, mixed_ref, *refs):
    query_refs, out_ref = refs[:-1], refs[-1]
    groups, rows, width = out_ref.shape
    pair = 2
    for k in range(0, groups, pair):
        for h in range(width // HEAD_DIM):
            cols = head_cols(h)
            queries = jnp.concatenate([ref[:, cols] for ref in query_refs[k : k + pair]], axis=0)
            scores = dot_nt(queries, mixed_ref[:, cols])
            peak = jnp.max(scores, axis=1, keepdims=True)
            weights = jnp.exp2((scores - peak) * EXP2_SCALE)
            den = jnp.sum(weights, axis=1, keepdims=True)
            result = jnp.dot(
                weights.astype(jnp.bfloat16), mixed_ref[:, cols], preferred_element_type=jnp.float32
            )
            result = result / den
            for p in range(pair):
                at = (place_ref[0] + groups - k - p) % groups
                out_ref[at, :, cols] = result[p * rows : (p + 1) * rows]


def decode(place, mixed, queries):
    rows, width = queries[0].shape
    shape = (len(queries), rows, width)
    return pl.pallas_call(
        decode_body,
        grid=(1,),
        in_specs=[pl.BlockSpec(memory_space=pltpu.SMEM)]
        + [whole_spec(block) for block in (mixed,) + queries],
        out_specs=pl.BlockSpec(shape, lambda i: (0, 0, 0)),
        out_shape=jax.ShapeDtypeStruct(shape, jnp.float32),
        compiler_params=pltpu.CompilerParams(vmem_limit_bytes=VMEM_BYTES),
        interpret=INTERPRET,
        name="decode",
    )(place, mixed, *queries)


def scalar(index):
    return index.reshape(1).astype(jnp.int32)


def join(first, second):
    return jnp.concatenate([first, second], axis=0)


def all_to_all(block, axis):
    return lax.all_to_all(block, axis, 0, 0, tiled=True)


def local(inputs, kv_weight, latent_queries, mix_gain, mix_weight, output_queries):
    groups = lax.axis_size("x")
    members = lax.axis_size("z")
    place = lax.axis_index("x")
    core_index = lax.axis_index("core")
    core = scalar(core_index)
    latent_width = HEADS * HEAD_DIM
    width = latent_width // groups

    mine = inputs[0]
    half = mine.shape[0] // 2
    above = shift(mine, "x", -1)
    below = shift(mine, "x", 1)

    mix_t = mix_weight.T
    mix_half = mix_t.shape[1] // 2
    held = lax.dynamic_slice_in_dim(mix_t, core_index * mix_half, mix_half, axis=1)
    for mask in XORS[:-1]:
        held = join(held, across(held, "z", mask))
    brought = across(held, "z", XORS[-1])

    rows = latent_queries.shape[0] // 2
    asked = lax.dynamic_slice_in_dim(latent_queries, core_index * rows, rows, axis=0)
    asked = jnp.stack([asked[:, g * width : (g + 1) * width] for g in range(groups)], axis=0)
    asked = jnp.broadcast_to(asked[:, None], (groups, members, rows, width))
    asked = asked.reshape(groups * members, rows, width)
    asked = all_to_all(asked, ("x", "z"))
    asked = asked.reshape(groups * members * rows, width)
    asked_other = partner(asked)

    far_low = above[:half]
    far_low = shift(far_low, "x", -1)
    far_high = below[half:]
    far_high = shift(far_high, "x", 1)
    weight = jnp.concatenate(
        [
            lax.dynamic_slice_in_dim(kv_weight, place * width, width, axis=1),
            lax.dynamic_slice_in_dim(kv_weight, latent_width + place * width, width, axis=1),
        ],
        axis=1,
    )
    latents = groups * members * rows * 2
    parts = attend(
        core,
        asked,
        asked_other,
        weight,
        (mine, above, below, far_low, far_high),
        members,
        latents // 4,
    )
    parts = all_to_all(parts, "z")

    queries = []
    for k in range(groups):
        to = (place + k) % groups
        sent = lax.dynamic_slice_in_dim(output_queries[0], to * width, width, axis=1)
        queries.append(shift(sent, "x", k) if k else sent)
    mix_mine = order(scalar(lax.axis_index("z")), held, brought)
    mix_other = partner(mix_mine)

    window = all_to_all(combine(parts, groups), "x")
    own, one, two = products(core, window, mix_gain[None], mix_mine, mix_other)
    one = from_behind(one, FRAME, 1)
    two = from_behind(two, FRAME, 2)
    mixed = finish(own, one, two, members, 3 * latent_width)
    mixed = all_to_all(mixed, "z").reshape(latents, width)

    decoded = decode(scalar(place), mixed, tuple(queries))
    decoded = all_to_all(decoded, "x")
    return jnp.concatenate([decoded[g] for g in range(groups)], axis=1)[None]


def solution(mesh):
    grid = Mesh(mesh.devices.reshape(8, 2, 4, 8), ("y", "core", "x", "z"))
    tok = ("x", "z")
    return jax.shard_map(
        local,
        mesh=grid,
        in_specs=(P(FRAME, tok, None), P(), P(tok, None), P(), P(None, tok), P(FRAME, tok, None)),
        out_specs=P(FRAME, tok, None),
        check_vma=False,
    )
```

```python
import math

import jax
import jax.numpy as jnp
from jax import lax
from jax.experimental import pallas as pl
from jax.experimental.pallas import tpu as pltpu
from jax.sharding import Mesh
from jax.sharding import PartitionSpec as P


HEADS = 8
HEAD_DIM = 128
EXP2_SCALE = math.log2(math.e) / math.sqrt(HEAD_DIM)
FRAME = ("y", "core")
EXTRA = 8
TAIL = 8
VMEM_BYTES = 20 * 1024 * 1024
INTERPRET = False


def shift(block, axis, distance):
    size = lax.axis_size(axis)
    return lax.ppermute(block, axis, [(i, (i + distance) % size) for i in range(size)])


def from_behind(block, axis, distance):
    devices = range(lax.axis_size(axis))
    route = [(i - distance, i) for i in devices if i - distance in devices]
    return lax.ppermute(block, axis, route)


def partner(block):
    return lax.ppermute(block, "core", [(0, 1), (1, 0)])


def dot_nt(a, b):
    return lax.dot_general(a, b, (((1,), (1,)), ((), ())), preferred_element_type=jnp.float32)


def whole_spec(block):
    return pl.BlockSpec(block.shape, lambda i: (0,) * len(block.shape))


def head_cols(h):
    return slice(h * HEAD_DIM, (h + 1) * HEAD_DIM)


def project_inputs(in_refs, w_refs, kv_ref):
    low = 0
    for in_ref in in_refs:
        rows = in_ref.shape[0]
        left = 0
        for w_ref in w_refs:
            width = w_ref.shape[1]
            kv_ref[low : low + rows, left : left + width] = jnp.dot(
                in_ref[...], w_ref[...], preferred_element_type=jnp.float32
            ).astype(jnp.bfloat16)
            left += width
        low += rows


def pick_queries(spot_ref, mine_ref, other_ref, tile_ref):
    step = pl.program_id(0)
    tile = tile_ref.shape[0]
    per_half = mine_ref.shape[0] // tile
    start = pl.multiple_of((step % per_half) * tile, tile)
    is_mine = step // per_half == spot_ref[0]

    @pl.when(is_mine)
    def _():
        tile_ref[...] = mine_ref[pl.ds(start, tile), :]

    @pl.when(jnp.logical_not(is_mine))
    def _():
        tile_ref[...] = other_ref[pl.ds(start, tile), :]


def lanes(values, shape):
    lane = lax.broadcasted_iota(jnp.int32, shape, 1)
    result = jnp.broadcast_to(values[-1], shape)
    for k in range(len(values) - 2, -1, -1):
        result = jnp.where(lane == k, values[k], result)
    return result


def attend_body(spot_ref, mine_ref, other_ref, key_ref, value_ref, *refs):
    in_refs, (out_ref, kv_ref, q_ref) = refs[:-3], refs[-3:]
    width = mine_ref.shape[1]

    @pl.when(pl.program_id(0) == 0)
    def _():
        project_inputs(in_refs, (key_ref, value_ref), kv_ref)

    pick_queries(spot_ref, mine_ref, other_ref, q_ref)
    tile = q_ref.shape[0]
    blocks = out_ref.shape[0]
    rows = tile // blocks
    for h in range(width // HEAD_DIM):
        cols = head_cols(h)
        scores = dot_nt(q_ref[:, cols], kv_ref[:, cols])
        peak = jnp.max(scores, axis=1, keepdims=True)
        weights = jnp.exp2((scores - peak) * EXP2_SCALE)
        den = jnp.sum(weights, axis=1, keepdims=True)
        value_cols = slice(width + h * HEAD_DIM, width + (h + 1) * HEAD_DIM)
        num = jnp.dot(
            weights.astype(jnp.bfloat16), kv_ref[:, value_cols], preferred_element_type=jnp.float32
        )
        first = peak.astype(jnp.bfloat16).astype(jnp.float32)
        second = (peak - first).astype(jnp.bfloat16).astype(jnp.float32)
        packed = lanes([first, second, peak - first - second, den], (tile, HEAD_DIM)).T
        for b in range(blocks):
            span = slice(b * rows, (b + 1) * rows)
            out_ref[b, :rows, cols] = num[span].astype(jnp.bfloat16)
            out_ref[b, rows:, cols] = packed[:EXTRA, span].astype(jnp.bfloat16)


def attend(spot, mine, other, kv_weight, inputs, groups, blocks, tile):
    half, width = mine.shape
    latents = 2 * half
    rows = latents // blocks

    def still(block):
        return pl.BlockSpec(block.shape, lambda i, spot_ref: (0, 0))

    if not INTERPRET:
        kv_weight = pltpu.with_memory_space_constraint(kv_weight, pltpu.HBM)
    depth = kv_weight.shape[0]
    keys = pl.BlockSpec((depth, width), lambda i, spot_ref: (0, spot_ref[1]))
    values = pl.BlockSpec((depth, width), lambda i, spot_ref: (0, groups + spot_ref[1]))
    return pl.pallas_call(
        attend_body,
        grid_spec=pltpu.PrefetchScalarGridSpec(
            num_scalar_prefetch=1,
            grid=(latents // tile,),
            in_specs=[still(mine), still(other), keys, values] + [still(b) for b in inputs],
            out_specs=pl.BlockSpec(
                (tile // rows, rows + EXTRA, width), lambda i, spot_ref: (i, 0, 0)
            ),
            scratch_shapes=[
                pltpu.VMEM((sum(b.shape[0] for b in inputs), 2 * width), jnp.bfloat16),
                pltpu.VMEM((tile, width), jnp.bfloat16),
            ],
        ),
        out_shape=jax.ShapeDtypeStruct((blocks, rows + EXTRA, width), jnp.bfloat16),
        compiler_params=pltpu.CompilerParams(vmem_limit_bytes=VMEM_BYTES),
        interpret=INTERPRET,
        name="attend",
    )(spot, mine, other, kv_weight, kv_weight, *inputs)


def combine_body(part_ref, out_ref):
    blocks, height, width = part_ref.shape
    rows = height - EXTRA
    groups = out_ref.shape[0]
    peaks = []
    dens = []
    for b in range(blocks):
        extra = part_ref[b, rows:, :].astype(jnp.float32)
        peaks.append(extra[0:1] + extra[1:2] + extra[2:3])
        dens.append(extra[3:4])
    top = peaks[0]
    for peak in peaks[1:]:
        top = jnp.maximum(top, peak)
    scales = [jnp.exp2((peak - top) * EXP2_SCALE) for peak in peaks]
    den = scales[0] * dens[0]
    for scale, part in zip(scales[1:], dens[1:]):
        den = den + scale * part
    pad = jnp.zeros((HEAD_DIM - blocks - 1, width), jnp.float32)
    table = jnp.concatenate(scales + [den, pad], axis=0)
    for h in range(width // HEAD_DIM):
        cols = head_cols(h)
        turned = table[:, cols].T
        total = jnp.zeros((rows, HEAD_DIM), jnp.float32)
        for b in range(blocks):
            total = total + part_ref[b, :rows, cols].astype(jnp.float32) * turned[:, b : b + 1]
        latents = (total / turned[:, blocks : blocks + 1]).astype(jnp.bfloat16)
        for g in range(groups):
            out_ref[g, :, cols] = latents


def combine(parts, groups):
    _, height, width = parts.shape
    rows = height - EXTRA
    return pl.pallas_call(
        combine_body,
        grid=(1,),
        in_specs=[whole_spec(parts)],
        out_specs=pl.BlockSpec((groups, rows, width), lambda i: (0, 0, 0)),
        out_shape=jax.ShapeDtypeStruct((groups, rows, width), jnp.bfloat16),
        compiler_params=pltpu.CompilerParams(vmem_limit_bytes=VMEM_BYTES // 2),
        interpret=INTERPRET,
        name="combine",
    )(parts)


def turn(column):
    return jnp.broadcast_to(column, (column.shape[0], HEAD_DIM)).T


def products_body(core_ref, rows_ref, gain_ref, mine_ref, other_ref, own_ref, one_ref, two_ref):
    groups, _, width = rows_ref.shape
    full = groups * width
    half = mine_ref.shape[1]
    count = own_ref.shape[0] - TAIL
    squares = jnp.zeros((count, 1), jnp.float32)
    for g in range(groups):
        block = rows_ref[g].astype(jnp.float32)
        squares = squares + jnp.sum(block * block, axis=1, keepdims=True)
    tail = turn(squares)[:TAIL]
    outs = (own_ref, one_ref, two_ref)
    for out_ref in outs:
        for h in range(width // HEAD_DIM):
            out_ref[count:, head_cols(h)] = tail

    def multiply(halves):
        for t, out_ref in enumerate(outs):
            total = jnp.zeros((count, width), jnp.float32)
            for g in range(groups):
                low = t * full + g * width
                block = rows_ref[g].astype(jnp.float32) * gain_ref[:, low : low + width]
                part_ref = halves[low // half]
                at = low % half
                total = total + dot_nt(block.astype(jnp.bfloat16), part_ref[:, at : at + width])
            out_ref[:count, :] = total

    @pl.when(core_ref[0] == 0)
    def _():
        multiply((mine_ref, other_ref))

    @pl.when(core_ref[0] != 0)
    def _():
        multiply((other_ref, mine_ref))


def products(core, window, gain, mine, other):
    _, count, width = window.shape
    return pl.pallas_call(
        products_body,
        grid=(1,),
        in_specs=[
            pl.BlockSpec(memory_space=pltpu.SMEM),
        ]
        + [whole_spec(block) for block in (window, gain, mine, other)],
        out_specs=(pl.BlockSpec((count + TAIL, width), lambda i: (0, 0)),) * 3,
        out_shape=(jax.ShapeDtypeStruct((count + TAIL, width), jnp.float32),) * 3,
        compiler_params=pltpu.CompilerParams(vmem_limit_bytes=VMEM_BYTES),
        interpret=INTERPRET,
        name="products",
    )(core, window, gain, mine, other)


def finish_body(own_ref, one_ref, two_ref, out_ref, *, features):
    members, count, width = out_ref.shape
    squares = own_ref[count:, :] + one_ref[count:, :] + two_ref[count:, :]
    inverse = lax.rsqrt(squares / features + 1e-06)
    for h in range(width // HEAD_DIM):
        cols = head_cols(h)
        pad = jnp.zeros((HEAD_DIM - TAIL, HEAD_DIM), jnp.float32)
        column = jnp.concatenate([inverse[:, cols], pad], axis=0).T[:, :1]
        product = own_ref[:count, cols] + one_ref[:count, cols] + two_ref[:count, cols]
        value = product * column
        mixed = (0.5 * value * (1.0 + lax.erf(value * math.sqrt(0.5)))).astype(jnp.bfloat16)
        for m in range(members):
            out_ref[m, :, cols] = mixed


def finish(own, one, two, members, features):
    height, width = own.shape
    return pl.pallas_call(
        lambda *refs: finish_body(*refs, features=features),
        grid=(1,),
        in_specs=[whole_spec(own), whole_spec(one), whole_spec(two)],
        out_specs=pl.BlockSpec((members, height - TAIL, width), lambda i: (0, 0, 0)),
        out_shape=jax.ShapeDtypeStruct((members, height - TAIL, width), jnp.bfloat16),
        compiler_params=pltpu.CompilerParams(vmem_limit_bytes=VMEM_BYTES // 2),
        interpret=INTERPRET,
        name="finish",
    )(own, one, two)


def decode_body(place_ref, mixed_ref, query_ref, out_ref):
    groups, rows, width = out_ref.shape
    pair = 2
    for k in range(0, groups, pair):
        for h in range(width // HEAD_DIM):
            cols = head_cols(h)
            queries = query_ref[k * rows : (k + pair) * rows, cols]
            scores = dot_nt(queries, mixed_ref[:, cols])
            peak = jnp.max(scores, axis=1, keepdims=True)
            weights = jnp.exp2((scores - peak) * EXP2_SCALE)
            den = jnp.sum(weights, axis=1, keepdims=True)
            result = jnp.dot(
                weights.astype(jnp.bfloat16), mixed_ref[:, cols], preferred_element_type=jnp.float32
            )
            result = result / den
            for p in range(pair):
                at = (place_ref[0] + groups - k - p) % groups
                out_ref[at, :, cols] = result[p * rows : (p + 1) * rows]


def decode(place, mixed, queries, groups):
    count, width = queries.shape
    shape = (groups, count // groups, width)
    return pl.pallas_call(
        decode_body,
        grid=(1,),
        in_specs=[
            pl.BlockSpec(memory_space=pltpu.SMEM),
            whole_spec(mixed),
            whole_spec(queries),
        ],
        out_specs=pl.BlockSpec(shape, lambda i: (0, 0, 0)),
        out_shape=jax.ShapeDtypeStruct(shape, jnp.float32),
        compiler_params=pltpu.CompilerParams(vmem_limit_bytes=VMEM_BYTES),
        interpret=INTERPRET,
        name="decode",
    )(place, mixed, queries)


def scalar(index):
    return index.reshape(1).astype(jnp.int32)


def join(*blocks):
    return jnp.concatenate(blocks, axis=0)


def all_to_all(block, axis):
    return lax.all_to_all(block, axis, 0, 0, tiled=True)


def local(inputs, kv_weight, latent_queries, mix_gain, mix_weight, output_queries):
    groups = lax.axis_size("x")
    members = lax.axis_size("z")
    place = lax.axis_index("x")
    core_index = lax.axis_index("core")
    core = scalar(core_index)
    latent_width = HEADS * HEAD_DIM
    width = latent_width // groups

    mine = inputs[0]
    half = mine.shape[0] // 2
    above = shift(mine, "x", -1)
    below = shift(mine, "x", 1)

    mix_t = mix_weight.T
    mix_half = mix_t.shape[1] // 2
    mix_mine = lax.dynamic_slice_in_dim(mix_t, core_index * mix_half, mix_half, axis=1)
    mix_mine = jnp.broadcast_to(mix_mine[None], (members,) + mix_mine.shape)
    mix_mine = all_to_all(mix_mine, "z")
    mix_mine = mix_mine.reshape(members * mix_t.shape[0], mix_half)
    mix_other = partner(mix_mine)

    rows = latent_queries.shape[0] // 2
    asked = lax.dynamic_slice_in_dim(latent_queries, core_index * rows, rows, axis=0)
    asked = jnp.stack([asked[:, g * width : (g + 1) * width] for g in range(groups)], axis=0)
    asked = jnp.broadcast_to(asked[:, None], (groups, members, rows, width))
    asked = asked.reshape(groups * members, rows, width)
    asked = all_to_all(asked, ("x", "z"))
    asked = asked.reshape(groups * members * rows, width)
    asked_other = partner(asked)

    far_low = above[:half]
    far_low = shift(far_low, "x", -1)
    far_high = below[half:]
    far_high = shift(far_high, "x", 1)
    latents = groups * members * rows * 2
    parts = attend(
        jnp.stack([core_index, place]).astype(jnp.int32),
        asked,
        asked_other,
        kv_weight,
        (mine, above, below, far_low, far_high),
        groups,
        members,
        latents // 4,
    )
    parts = all_to_all(parts, "z")

    queries = []
    for k in range(groups):
        to = (place + k) % groups
        sent = lax.dynamic_slice_in_dim(output_queries[0], to * width, width, axis=1)
        queries.append(shift(sent, "x", k) if k else sent)
    sent = lax.optimization_barrier(join(*queries[1:]))

    window = all_to_all(combine(parts, groups), "x")
    own, one, two = products(core, window, mix_gain[None], mix_mine, mix_other)
    one = from_behind(one, FRAME, 1)
    two = from_behind(two, FRAME, 2)
    mixed = finish(own, one, two, members, 3 * latent_width)
    mixed = all_to_all(mixed, "z").reshape(latents, width)
    queries = join(queries[0], sent)

    decoded = decode(scalar(place), mixed, queries, groups)
    decoded = all_to_all(decoded, "x")
    return jnp.concatenate([decoded[g] for g in range(groups)], axis=1)[None]


def solution(mesh):
    grid = Mesh(mesh.devices.reshape(8, 2, 4, 8), ("y", "core", "x", "z"))
    tok = ("x", "z")
    return jax.shard_map(
        local,
        mesh=grid,
        in_specs=(P(FRAME, tok, None), P(), P(tok, None), P(), P(None, tok), P(FRAME, tok, None)),
        out_specs=P(FRAME, tok, None),
        check_vma=False,
    )
```

```python
import math

import jax
import jax.numpy as jnp
from jax import lax
from jax.experimental import pallas as pl
from jax.experimental.pallas import tpu as pltpu
from jax.sharding import Mesh
from jax.sharding import PartitionSpec as P


HEADS = 8
HEAD_DIM = 128
EXP2_SCALE = math.log2(math.e) / math.sqrt(HEAD_DIM)
FRAME = ("y", "core")
EXTRA = 8
TAIL = 8
XORS = (4, 2, 1)
MASKS = (0, 4, 2, 6, 1, 5, 3, 7)
VMEM_BYTES = 20 * 1024 * 1024
INTERPRET = False


def shift(block, axis, distance):
    size = lax.axis_size(axis)
    return lax.ppermute(block, axis, [(i, (i + distance) % size) for i in range(size)])


def from_behind(block, axis, distance):
    devices = range(lax.axis_size(axis))
    route = [(i - distance, i) for i in devices if i - distance in devices]
    return lax.ppermute(block, axis, route)


def across(block, axis, mask):
    return lax.ppermute(block, axis, [(i, i ^ mask) for i in range(lax.axis_size(axis))])


def partner(block):
    return lax.ppermute(block, "core", [(0, 1), (1, 0)])


def dot_nt(a, b):
    return lax.dot_general(a, b, (((1,), (1,)), ((), ())), preferred_element_type=jnp.float32)


def whole_spec(block):
    return pl.BlockSpec(block.shape, lambda i: (0,) * len(block.shape))


def head_cols(h):
    return slice(h * HEAD_DIM, (h + 1) * HEAD_DIM)


def project_inputs(in_refs, w_refs, kv_ref):
    low = 0
    for in_ref in in_refs:
        rows = in_ref.shape[0]
        left = 0
        for w_ref in w_refs:
            width = w_ref.shape[1]
            kv_ref[low : low + rows, left : left + width] = jnp.dot(
                in_ref[...], w_ref[...], preferred_element_type=jnp.float32
            ).astype(jnp.bfloat16)
            left += width
        low += rows


def pick_queries(spot_ref, mine_ref, other_ref, tile_ref):
    step = pl.program_id(0)
    tile = tile_ref.shape[0]
    per_half = mine_ref.shape[0] // tile
    start = pl.multiple_of((step % per_half) * tile, tile)
    is_mine = step // per_half == spot_ref[0]

    @pl.when(is_mine)
    def _():
        tile_ref[...] = mine_ref[pl.ds(start, tile), :]

    @pl.when(jnp.logical_not(is_mine))
    def _():
        tile_ref[...] = other_ref[pl.ds(start, tile), :]


def lanes(values, shape):
    lane = lax.broadcasted_iota(jnp.int32, shape, 1)
    result = jnp.broadcast_to(values[-1], shape)
    for k in range(len(values) - 2, -1, -1):
        result = jnp.where(lane == k, values[k], result)
    return result


def attend_body(spot_ref, mine_ref, other_ref, key_ref, value_ref, *refs):
    in_refs, (out_ref, kv_ref, q_ref) = refs[:-3], refs[-3:]
    width = mine_ref.shape[1]

    @pl.when(pl.program_id(0) == 0)
    def _():
        project_inputs(in_refs, (key_ref, value_ref), kv_ref)

    pick_queries(spot_ref, mine_ref, other_ref, q_ref)
    tile = q_ref.shape[0]
    blocks = out_ref.shape[0]
    rows = tile // blocks
    for h in range(width // HEAD_DIM):
        cols = head_cols(h)
        scores = dot_nt(q_ref[:, cols], kv_ref[:, cols])
        peak = jnp.max(scores, axis=1, keepdims=True)
        weights = jnp.exp2((scores - peak) * EXP2_SCALE)
        den = jnp.sum(weights, axis=1, keepdims=True)
        value_cols = slice(width + h * HEAD_DIM, width + (h + 1) * HEAD_DIM)
        num = jnp.dot(
            weights.astype(jnp.bfloat16), kv_ref[:, value_cols], preferred_element_type=jnp.float32
        )
        first = peak.astype(jnp.bfloat16).astype(jnp.float32)
        second = (peak - first).astype(jnp.bfloat16).astype(jnp.float32)
        packed = lanes([first, second, peak - first - second, den], (tile, HEAD_DIM)).T
        for b in range(blocks):
            span = slice(b * rows, (b + 1) * rows)
            out_ref[b, :rows, cols] = num[span].astype(jnp.bfloat16)
            out_ref[b, rows:, cols] = packed[:EXTRA, span].astype(jnp.bfloat16)


def attend(spot, mine, other, kv_weight, inputs, groups, blocks, tile):
    half, width = mine.shape
    latents = 2 * half
    rows = latents // blocks

    def still(block):
        return pl.BlockSpec(block.shape, lambda i, spot_ref: (0, 0))

    if not INTERPRET:
        kv_weight = pltpu.with_memory_space_constraint(kv_weight, pltpu.HBM)
    depth = kv_weight.shape[0]
    keys = pl.BlockSpec((depth, width), lambda i, spot_ref: (0, spot_ref[1]))
    values = pl.BlockSpec((depth, width), lambda i, spot_ref: (0, groups + spot_ref[1]))
    return pl.pallas_call(
        attend_body,
        grid_spec=pltpu.PrefetchScalarGridSpec(
            num_scalar_prefetch=1,
            grid=(latents // tile,),
            in_specs=[still(mine), still(other), keys, values] + [still(b) for b in inputs],
            out_specs=pl.BlockSpec(
                (tile // rows, rows + EXTRA, width), lambda i, spot_ref: (i, 0, 0)
            ),
            scratch_shapes=[
                pltpu.VMEM((sum(b.shape[0] for b in inputs), 2 * width), jnp.bfloat16),
                pltpu.VMEM((tile, width), jnp.bfloat16),
            ],
        ),
        out_shape=jax.ShapeDtypeStruct((blocks, rows + EXTRA, width), jnp.bfloat16),
        compiler_params=pltpu.CompilerParams(vmem_limit_bytes=VMEM_BYTES),
        interpret=INTERPRET,
        name="attend",
    )(spot, mine, other, kv_weight, kv_weight, *inputs)


def order_body(place_ref, first_ref, second_ref, out_ref):
    rows = out_ref.shape[0] // len(MASKS)
    half = len(MASKS) // 2
    for j, mask in enumerate(MASKS):
        part_ref = (first_ref, second_ref)[j // half]
        low = (j % half) * rows
        at = pl.multiple_of((place_ref[0] ^ mask) * rows, rows)
        out_ref[pl.ds(at, rows), :] = part_ref[low : low + rows, :]


def order(place, first, second):
    shape = (2 * first.shape[0], first.shape[1])
    return pl.pallas_call(
        order_body,
        grid=(1,),
        in_specs=[pl.BlockSpec(memory_space=pltpu.SMEM), whole_spec(first), whole_spec(second)],
        out_specs=pl.BlockSpec(shape, lambda i: (0, 0)),
        out_shape=jax.ShapeDtypeStruct(shape, first.dtype),
        compiler_params=pltpu.CompilerParams(vmem_limit_bytes=VMEM_BYTES // 2),
        interpret=INTERPRET,
        name="order",
    )(place, first, second)


def combine_body(part_ref, out_ref):
    blocks, height, width = part_ref.shape
    rows = height - EXTRA
    groups = out_ref.shape[0]
    peaks = []
    dens = []
    for b in range(blocks):
        extra = part_ref[b, rows:, :].astype(jnp.float32)
        peaks.append(extra[0:1] + extra[1:2] + extra[2:3])
        dens.append(extra[3:4])
    top = peaks[0]
    for peak in peaks[1:]:
        top = jnp.maximum(top, peak)
    scales = [jnp.exp2((peak - top) * EXP2_SCALE) for peak in peaks]
    den = scales[0] * dens[0]
    for scale, part in zip(scales[1:], dens[1:]):
        den = den + scale * part
    pad = jnp.zeros((HEAD_DIM - blocks - 1, width), jnp.float32)
    table = jnp.concatenate(scales + [den, pad], axis=0)
    for h in range(width // HEAD_DIM):
        cols = head_cols(h)
        turned = table[:, cols].T
        total = jnp.zeros((rows, HEAD_DIM), jnp.float32)
        for b in range(blocks):
            total = total + part_ref[b, :rows, cols].astype(jnp.float32) * turned[:, b : b + 1]
        latents = (total / turned[:, blocks : blocks + 1]).astype(jnp.bfloat16)
        for g in range(groups):
            out_ref[g, :, cols] = latents


def combine(parts, groups):
    _, height, width = parts.shape
    rows = height - EXTRA
    return pl.pallas_call(
        combine_body,
        grid=(1,),
        in_specs=[whole_spec(parts)],
        out_specs=pl.BlockSpec((groups, rows, width), lambda i: (0, 0, 0)),
        out_shape=jax.ShapeDtypeStruct((groups, rows, width), jnp.bfloat16),
        compiler_params=pltpu.CompilerParams(vmem_limit_bytes=VMEM_BYTES // 2),
        interpret=INTERPRET,
        name="combine",
    )(parts)


def turn(column):
    return jnp.broadcast_to(column, (column.shape[0], HEAD_DIM)).T


def products_body(core_ref, rows_ref, gain_ref, mine_ref, other_ref, own_ref, one_ref, two_ref):
    groups, _, width = rows_ref.shape
    full = groups * width
    half = mine_ref.shape[1]
    count = own_ref.shape[0] - TAIL
    squares = jnp.zeros((count, 1), jnp.float32)
    for g in range(groups):
        block = rows_ref[g].astype(jnp.float32)
        squares = squares + jnp.sum(block * block, axis=1, keepdims=True)
    tail = turn(squares)[:TAIL]
    outs = (own_ref, one_ref, two_ref)
    for out_ref in outs:
        for h in range(width // HEAD_DIM):
            out_ref[count:, head_cols(h)] = tail

    def multiply(halves):
        for t, out_ref in enumerate(outs):
            total = jnp.zeros((count, width), jnp.float32)
            for g in range(groups):
                low = t * full + g * width
                block = rows_ref[g].astype(jnp.float32) * gain_ref[:, low : low + width]
                part_ref = halves[low // half]
                at = low % half
                total = total + dot_nt(block.astype(jnp.bfloat16), part_ref[:, at : at + width])
            out_ref[:count, :] = total

    @pl.when(core_ref[0] == 0)
    def _():
        multiply((mine_ref, other_ref))

    @pl.when(core_ref[0] != 0)
    def _():
        multiply((other_ref, mine_ref))


def products(core, window, gain, mine, other):
    _, count, width = window.shape
    return pl.pallas_call(
        products_body,
        grid=(1,),
        in_specs=[
            pl.BlockSpec(memory_space=pltpu.SMEM),
        ]
        + [whole_spec(block) for block in (window, gain, mine, other)],
        out_specs=(pl.BlockSpec((count + TAIL, width), lambda i: (0, 0)),) * 3,
        out_shape=(jax.ShapeDtypeStruct((count + TAIL, width), jnp.float32),) * 3,
        compiler_params=pltpu.CompilerParams(vmem_limit_bytes=VMEM_BYTES),
        interpret=INTERPRET,
        name="products",
    )(core, window, gain, mine, other)


def finish_body(own_ref, one_ref, two_ref, out_ref, *, features):
    members, count, width = out_ref.shape
    squares = own_ref[count:, :] + one_ref[count:, :] + two_ref[count:, :]
    inverse = lax.rsqrt(squares / features + 1e-06)
    for h in range(width // HEAD_DIM):
        cols = head_cols(h)
        pad = jnp.zeros((HEAD_DIM - TAIL, HEAD_DIM), jnp.float32)
        column = jnp.concatenate([inverse[:, cols], pad], axis=0).T[:, :1]
        product = own_ref[:count, cols] + one_ref[:count, cols] + two_ref[:count, cols]
        value = product * column
        mixed = (0.5 * value * (1.0 + lax.erf(value * math.sqrt(0.5)))).astype(jnp.bfloat16)
        for m in range(members):
            out_ref[m, :, cols] = mixed


def finish(own, one, two, members, features):
    height, width = own.shape
    return pl.pallas_call(
        lambda *refs: finish_body(*refs, features=features),
        grid=(1,),
        in_specs=[whole_spec(own), whole_spec(one), whole_spec(two)],
        out_specs=pl.BlockSpec((members, height - TAIL, width), lambda i: (0, 0, 0)),
        out_shape=jax.ShapeDtypeStruct((members, height - TAIL, width), jnp.bfloat16),
        compiler_params=pltpu.CompilerParams(vmem_limit_bytes=VMEM_BYTES // 2),
        interpret=INTERPRET,
        name="finish",
    )(own, one, two)


def decode_body(place_ref, mixed_ref, *refs):
    query_refs, out_ref = refs[:-1], refs[-1]
    groups, rows, width = out_ref.shape
    pair = 2
    for k in range(0, groups, pair):
        for h in range(width // HEAD_DIM):
            cols = head_cols(h)
            queries = jnp.concatenate([ref[:, cols] for ref in query_refs[k : k + pair]], axis=0)
            scores = dot_nt(queries, mixed_ref[:, cols])
            peak = jnp.max(scores, axis=1, keepdims=True)
            weights = jnp.exp2((scores - peak) * EXP2_SCALE)
            den = jnp.sum(weights, axis=1, keepdims=True)
            result = jnp.dot(
                weights.astype(jnp.bfloat16), mixed_ref[:, cols], preferred_element_type=jnp.float32
            )
            result = result / den
            for p in range(pair):
                at = (place_ref[0] + groups - k - p) % groups
                out_ref[at, :, cols] = result[p * rows : (p + 1) * rows]


def decode(place, mixed, queries):
    rows, width = queries[0].shape
    shape = (len(queries), rows, width)
    return pl.pallas_call(
        decode_body,
        grid=(1,),
        in_specs=[pl.BlockSpec(memory_space=pltpu.SMEM)]
        + [whole_spec(block) for block in (mixed,) + queries],
        out_specs=pl.BlockSpec(shape, lambda i: (0, 0, 0)),
        out_shape=jax.ShapeDtypeStruct(shape, jnp.float32),
        compiler_params=pltpu.CompilerParams(vmem_limit_bytes=VMEM_BYTES),
        interpret=INTERPRET,
        name="decode",
    )(place, mixed, *queries)


def scalar(index):
    return index.reshape(1).astype(jnp.int32)


def join(first, second):
    return jnp.concatenate([first, second], axis=0)


def all_to_all(block, axis):
    return lax.all_to_all(block, axis, 0, 0, tiled=True)


def local(inputs, kv_weight, latent_queries, mix_gain, mix_weight, output_queries):
    groups = lax.axis_size("x")
    members = lax.axis_size("z")
    place = lax.axis_index("x")
    core_index = lax.axis_index("core")
    core = scalar(core_index)
    latent_width = HEADS * HEAD_DIM
    width = latent_width // groups

    mine = inputs[0]
    half = mine.shape[0] // 2
    above = shift(mine, "x", -1)
    below = shift(mine, "x", 1)

    mix_t = mix_weight.T
    mix_half = mix_t.shape[1] // 2
    held = lax.dynamic_slice_in_dim(mix_t, core_index * mix_half, mix_half, axis=1)
    for mask in XORS[:-1]:
        held = join(held, across(held, "z", mask))
    brought = across(held, "z", XORS[-1])

    rows = latent_queries.shape[0] // 2
    asked = lax.dynamic_slice_in_dim(latent_queries, core_index * rows, rows, axis=0)
    asked = jnp.stack([asked[:, g * width : (g + 1) * width] for g in range(groups)], axis=0)
    asked = jnp.broadcast_to(asked[:, None], (groups, members, rows, width))
    asked = asked.reshape(groups * members, rows, width)
    asked = all_to_all(asked, ("x", "z"))
    asked = asked.reshape(groups * members * rows, width)
    asked_other = partner(asked)

    far_low = above[:half]
    far_low = shift(far_low, "x", -1)
    far_high = below[half:]
    far_high = shift(far_high, "x", 1)
    latents = groups * members * rows * 2
    parts = attend(
        jnp.stack([core_index, place]).astype(jnp.int32),
        asked,
        asked_other,
        kv_weight,
        (mine, above, below, far_low, far_high),
        groups,
        members,
        latents // 4,
    )
    parts = all_to_all(parts, "z")

    queries = []
    for k in range(groups):
        to = (place + k) % groups
        sent = lax.dynamic_slice_in_dim(output_queries[0], to * width, width, axis=1)
        queries.append(shift(sent, "x", k) if k else sent)
    mix_mine = order(scalar(lax.axis_index("z")), held, brought)
    mix_other = partner(mix_mine)

    window = all_to_all(combine(parts, groups), "x")
    own, one, two = products(core, window, mix_gain[None], mix_mine, mix_other)
    one = from_behind(one, FRAME, 1)
    two = from_behind(two, FRAME, 2)
    mixed = finish(own, one, two, members, 3 * latent_width)
    mixed = all_to_all(mixed, "z").reshape(latents, width)

    decoded = decode(scalar(place), mixed, tuple(queries))
    decoded = all_to_all(decoded, "x")
    return jnp.concatenate([decoded[g] for g in range(groups)], axis=1)[None]


def solution(mesh):
    grid = Mesh(mesh.devices.reshape(8, 2, 4, 8), ("y", "core", "x", "z"))
    tok = ("x", "z")
    return jax.shard_map(
        local,
        mesh=grid,
        in_specs=(P(FRAME, tok, None), P(), P(tok, None), P(), P(None, tok), P(FRAME, tok, None)),
        out_specs=P(FRAME, tok, None),
        check_vma=False,
    )
```

```python
import math

import jax
import jax.numpy as jnp
from jax import lax
from jax.experimental import pallas as pl
from jax.experimental.pallas import tpu as pltpu
from jax.sharding import Mesh
from jax.sharding import PartitionSpec as P


HEADS = 8
HEAD_DIM = 128
EXP2_SCALE = math.log2(math.e) / math.sqrt(HEAD_DIM)
FRAME = ("y", "core")
EXTRA = 8
CHUNK = 768
TAIL = 8
XORS = (4, 2, 1)
MASKS = (0, 4, 2, 6, 1, 5, 3, 7)
VMEM_BYTES = 20 * 1024 * 1024
INTERPRET = False


def shift(block, axis, distance):
    size = lax.axis_size(axis)
    return lax.ppermute(block, axis, [(i, (i + distance) % size) for i in range(size)])


def from_behind(block, axis, distance):
    devices = range(lax.axis_size(axis))
    route = [(i - distance, i) for i in devices if i - distance in devices]
    return lax.ppermute(block, axis, route)


def skew(block):
    ys, zs = lax.axis_size("y"), lax.axis_size("z")
    route = [(y * zs + (z ^ y), y * zs + z) for y in range(ys) for z in range(zs)]
    return lax.ppermute(block, ("y", "z"), route)


def across(block, axis, mask):
    return lax.ppermute(block, axis, [(i, i ^ mask) for i in range(lax.axis_size(axis))])


def partner(block):
    return lax.ppermute(block, "core", [(0, 1), (1, 0)])


def dot_nt(a, b):
    return lax.dot_general(a, b, (((1,), (1,)), ((), ())), preferred_element_type=jnp.float32)


def whole_spec(block):
    return pl.BlockSpec(block.shape, lambda i: (0,) * len(block.shape))


def head_cols(h):
    return slice(h * HEAD_DIM, (h + 1) * HEAD_DIM)


def project_inputs(in_refs, w_refs, kv_ref):
    low = 0
    for in_ref in in_refs:
        rows = in_ref.shape[0]
        left = 0
        for w_ref in w_refs:
            width = w_ref.shape[1]
            kv_ref[low : low + rows, left : left + width] = jnp.dot(
                in_ref[...], w_ref[...], preferred_element_type=jnp.float32
            ).astype(jnp.bfloat16)
            left += width
        low += rows


def pick_queries(spot_ref, mine_ref, other_ref, tile_ref):
    step = pl.program_id(0)
    tile = tile_ref.shape[0]
    per_half = mine_ref.shape[0] // tile
    start = pl.multiple_of((step % per_half) * tile, tile)
    is_mine = step // per_half == spot_ref[0]

    @pl.when(is_mine)
    def _():
        tile_ref[...] = mine_ref[pl.ds(start, tile), :]

    @pl.when(jnp.logical_not(is_mine))
    def _():
        tile_ref[...] = other_ref[pl.ds(start, tile), :]


def lanes(values, shape):
    lane = lax.broadcasted_iota(jnp.int32, shape, 1)
    result = jnp.broadcast_to(values[-1], shape)
    for k in range(len(values) - 2, -1, -1):
        result = jnp.where(lane == k, values[k], result)
    return result


def attend_body(spot_ref, mine_ref, other_ref, key_ref, value_ref, *refs):
    in_refs, (out_ref, kv_ref, q_ref) = refs[:-3], refs[-3:]
    width = mine_ref.shape[1]

    @pl.when(pl.program_id(0) == 0)
    def _():
        project_inputs(in_refs, (key_ref, value_ref), kv_ref)

    pick_queries(spot_ref, mine_ref, other_ref, q_ref)
    tile = q_ref.shape[0]
    blocks = out_ref.shape[0]
    rows = tile // blocks
    heads = range(width // HEAD_DIM)
    states = [None for _ in heads]
    count = kv_ref.shape[0]
    chunk = CHUNK if count % CHUNK == 0 else count
    for low in range(0, count, chunk):
        span = slice(low, low + chunk)
        for h in heads:
            scores = dot_nt(q_ref[:, head_cols(h)], kv_ref[span, head_cols(h)])
            peak = jnp.max(scores, axis=1, keepdims=True)
            if states[h] is not None:
                peak = jnp.maximum(peak, states[h][0])
            weights = jnp.exp2((scores - peak) * EXP2_SCALE)
            den = jnp.sum(weights, axis=1, keepdims=True)
            values = kv_ref[span, width + h * HEAD_DIM : width + (h + 1) * HEAD_DIM]
            num = jnp.dot(weights.astype(jnp.bfloat16), values, preferred_element_type=jnp.float32)
            if states[h] is not None:
                rescale = jnp.exp2((states[h][0] - peak) * EXP2_SCALE)
                den = den + rescale * states[h][1]
                num = num + rescale * states[h][2]
            states[h] = (peak, den, num)
    for h in heads:
        cols = head_cols(h)
        peak, den, num = states[h]
        first = peak.astype(jnp.bfloat16).astype(jnp.float32)
        second = (peak - first).astype(jnp.bfloat16).astype(jnp.float32)
        packed = lanes([first, second, peak - first - second, den], (tile, HEAD_DIM)).T
        for b in range(blocks):
            span = slice(b * rows, (b + 1) * rows)
            out_ref[b, :rows, cols] = num[span].astype(jnp.bfloat16)
            out_ref[b, rows:, cols] = packed[:EXTRA, span].astype(jnp.bfloat16)


def attend(spot, mine, other, kv_weight, inputs, groups, blocks, tile):
    half, width = mine.shape
    latents = 2 * half
    rows = latents // blocks

    def still(block):
        return pl.BlockSpec(block.shape, lambda i, spot_ref: (0, 0))

    if not INTERPRET:
        kv_weight = pltpu.with_memory_space_constraint(kv_weight, pltpu.HBM)
    depth = kv_weight.shape[0]
    keys = pl.BlockSpec((depth, width), lambda i, spot_ref: (0, spot_ref[1]))
    values = pl.BlockSpec((depth, width), lambda i, spot_ref: (0, groups + spot_ref[1]))
    return pl.pallas_call(
        attend_body,
        grid_spec=pltpu.PrefetchScalarGridSpec(
            num_scalar_prefetch=1,
            grid=(latents // tile,),
            in_specs=[still(mine), still(other), keys, values] + [still(b) for b in inputs],
            out_specs=pl.BlockSpec(
                (tile // rows, rows + EXTRA, width), lambda i, spot_ref: (i, 0, 0)
            ),
            scratch_shapes=[
                pltpu.VMEM((sum(b.shape[0] for b in inputs), 2 * width), jnp.bfloat16),
                pltpu.VMEM((tile, width), jnp.bfloat16),
            ],
        ),
        out_shape=jax.ShapeDtypeStruct((blocks, rows + EXTRA, width), jnp.bfloat16),
        compiler_params=pltpu.CompilerParams(vmem_limit_bytes=VMEM_BYTES),
        interpret=INTERPRET,
        name="attend",
    )(spot, mine, other, kv_weight, kv_weight, *inputs)


def order_body(place_ref, first_ref, second_ref, out_ref):
    rows = out_ref.shape[0] // len(MASKS)
    half = len(MASKS) // 2
    for j, mask in enumerate(MASKS):
        part_ref = (first_ref, second_ref)[j // half]
        low = (j % half) * rows
        at = pl.multiple_of((place_ref[0] ^ mask) * rows, rows)
        out_ref[pl.ds(at, rows), :] = part_ref[low : low + rows, :]


def order(place, first, second):
    shape = (2 * first.shape[0], first.shape[1])
    return pl.pallas_call(
        order_body,
        grid=(1,),
        in_specs=[pl.BlockSpec(memory_space=pltpu.SMEM), whole_spec(first), whole_spec(second)],
        out_specs=pl.BlockSpec(shape, lambda i: (0, 0)),
        out_shape=jax.ShapeDtypeStruct(shape, first.dtype),
        compiler_params=pltpu.CompilerParams(vmem_limit_bytes=VMEM_BYTES // 2),
        interpret=INTERPRET,
        name="order",
    )(place, first, second)


def combine_body(part_ref, out_ref):
    blocks, height, width = part_ref.shape
    rows = height - EXTRA
    groups = out_ref.shape[0]
    peaks = []
    dens = []
    for b in range(blocks):
        extra = part_ref[b, rows:, :].astype(jnp.float32)
        peaks.append(extra[0:1] + extra[1:2] + extra[2:3])
        dens.append(extra[3:4])
    top = peaks[0]
    for peak in peaks[1:]:
        top = jnp.maximum(top, peak)
    scales = [jnp.exp2((peak - top) * EXP2_SCALE) for peak in peaks]
    den = scales[0] * dens[0]
    for scale, part in zip(scales[1:], dens[1:]):
        den = den + scale * part
    pad = jnp.zeros((HEAD_DIM - blocks - 1, width), jnp.float32)
    table = jnp.concatenate(scales + [den, pad], axis=0)
    for h in range(width // HEAD_DIM):
        cols = head_cols(h)
        turned = table[:, cols].T
        total = jnp.zeros((rows, HEAD_DIM), jnp.float32)
        for b in range(blocks):
            total = total + part_ref[b, :rows, cols].astype(jnp.float32) * turned[:, b : b + 1]
        latents = (total / turned[:, blocks : blocks + 1]).astype(jnp.bfloat16)
        for g in range(groups):
            out_ref[g, :, cols] = latents


def combine(parts, groups):
    _, height, width = parts.shape
    rows = height - EXTRA
    return pl.pallas_call(
        combine_body,
        grid=(1,),
        in_specs=[whole_spec(parts)],
        out_specs=pl.BlockSpec((groups, rows, width), lambda i: (0, 0, 0)),
        out_shape=jax.ShapeDtypeStruct((groups, rows, width), jnp.bfloat16),
        compiler_params=pltpu.CompilerParams(vmem_limit_bytes=VMEM_BYTES // 2),
        interpret=INTERPRET,
        name="combine",
    )(parts)


def turn(column):
    return jnp.broadcast_to(column, (column.shape[0], HEAD_DIM)).T


def products_body(core_ref, rows_ref, gain_ref, mine_ref, other_ref, own_ref, one_ref, two_ref):
    groups, _, width = rows_ref.shape
    full = groups * width
    half = mine_ref.shape[1]
    count = own_ref.shape[0] - TAIL
    squares = jnp.zeros((count, 1), jnp.float32)
    for g in range(groups):
        block = rows_ref[g].astype(jnp.float32)
        squares = squares + jnp.sum(block * block, axis=1, keepdims=True)
    tail = turn(squares)[:TAIL]
    outs = (own_ref, one_ref, two_ref)
    for out_ref in outs:
        for h in range(width // HEAD_DIM):
            out_ref[count:, head_cols(h)] = tail

    def multiply(halves):
        for t, out_ref in enumerate(outs):
            total = jnp.zeros((count, width), jnp.float32)
            for g in range(groups):
                low = t * full + g * width
                block = rows_ref[g].astype(jnp.float32) * gain_ref[:, low : low + width]
                part_ref = halves[low // half]
                at = low % half
                total = total + dot_nt(block.astype(jnp.bfloat16), part_ref[:, at : at + width])
            out_ref[:count, :] = total

    @pl.when(core_ref[0] == 0)
    def _():
        multiply((mine_ref, other_ref))

    @pl.when(core_ref[0] != 0)
    def _():
        multiply((other_ref, mine_ref))


def products(core, window, gain, mine, other):
    _, count, width = window.shape
    return pl.pallas_call(
        products_body,
        grid=(1,),
        in_specs=[
            pl.BlockSpec(memory_space=pltpu.SMEM),
        ]
        + [whole_spec(block) for block in (window, gain, mine, other)],
        out_specs=(pl.BlockSpec((count + TAIL, width), lambda i: (0, 0)),) * 3,
        out_shape=(jax.ShapeDtypeStruct((count + TAIL, width), jnp.float32),) * 3,
        compiler_params=pltpu.CompilerParams(vmem_limit_bytes=VMEM_BYTES),
        interpret=INTERPRET,
        name="products",
    )(core, window, gain, mine, other)


def finish_body(own_ref, one_ref, two_ref, out_ref, *, features):
    members, count, width = out_ref.shape
    squares = own_ref[count:, :] + one_ref[count:, :] + two_ref[count:, :]
    inverse = lax.rsqrt(squares / features + 1e-06)
    for h in range(width // HEAD_DIM):
        cols = head_cols(h)
        pad = jnp.zeros((HEAD_DIM - TAIL, HEAD_DIM), jnp.float32)
        column = jnp.concatenate([inverse[:, cols], pad], axis=0).T[:, :1]
        product = own_ref[:count, cols] + one_ref[:count, cols] + two_ref[:count, cols]
        value = product * column
        mixed = (0.5 * value * (1.0 + lax.erf(value * math.sqrt(0.5)))).astype(jnp.bfloat16)
        for m in range(members):
            out_ref[m, :, cols] = mixed


def finish(own, one, two, members, features):
    height, width = own.shape
    return pl.pallas_call(
        lambda *refs: finish_body(*refs, features=features),
        grid=(1,),
        in_specs=[whole_spec(own), whole_spec(one), whole_spec(two)],
        out_specs=pl.BlockSpec((members, height - TAIL, width), lambda i: (0, 0, 0)),
        out_shape=jax.ShapeDtypeStruct((members, height - TAIL, width), jnp.bfloat16),
        compiler_params=pltpu.CompilerParams(vmem_limit_bytes=VMEM_BYTES // 2),
        interpret=INTERPRET,
        name="finish",
    )(own, one, two)


def decode_body(place_ref, mixed_ref, *refs):
    query_refs, out_ref = refs[:-1], refs[-1]
    groups, rows, width = out_ref.shape
    pair = 2
    for k in range(0, groups, pair):
        for h in range(width // HEAD_DIM):
            cols = head_cols(h)
            queries = jnp.concatenate([ref[:, cols] for ref in query_refs[k : k + pair]], axis=0)
            scores = dot_nt(queries, mixed_ref[:, cols])
            peak = jnp.max(scores, axis=1, keepdims=True)
            weights = jnp.exp2((scores - peak) * EXP2_SCALE)
            den = jnp.sum(weights, axis=1, keepdims=True)
            result = jnp.dot(
                weights.astype(jnp.bfloat16), mixed_ref[:, cols], preferred_element_type=jnp.float32
            )
            result = result / den
            for p in range(pair):
                at = (place_ref[0] + groups - k - p) % groups
                out_ref[at, :, cols] = result[p * rows : (p + 1) * rows]


def decode(place, mixed, queries):
    rows, width = queries[0].shape
    shape = (len(queries), rows, width)
    return pl.pallas_call(
        decode_body,
        grid=(1,),
        in_specs=[pl.BlockSpec(memory_space=pltpu.SMEM)]
        + [whole_spec(block) for block in (mixed,) + queries],
        out_specs=pl.BlockSpec(shape, lambda i: (0, 0, 0)),
        out_shape=jax.ShapeDtypeStruct(shape, jnp.float32),
        compiler_params=pltpu.CompilerParams(vmem_limit_bytes=VMEM_BYTES),
        interpret=INTERPRET,
        name="decode",
    )(place, mixed, *queries)


def scalar(index):
    return index.reshape(1).astype(jnp.int32)


def join(first, second):
    return jnp.concatenate([first, second], axis=0)


def all_to_all(block, axis):
    return lax.all_to_all(block, axis, 0, 0, tiled=True)


def local(inputs, kv_weight, latent_queries, mix_gain, mix_weight, output_queries):
    groups = lax.axis_size("x")
    members = lax.axis_size("z")
    place = lax.axis_index("x")
    core_index = lax.axis_index("core")
    core = scalar(core_index)
    latent_width = HEADS * HEAD_DIM
    width = latent_width // groups

    mine = inputs[0]
    half = mine.shape[0] // 2
    above = shift(mine, "x", -1)
    below = shift(mine, "x", 1)

    mix_t = mix_weight.T
    mix_half = mix_t.shape[1] // 2
    held = lax.dynamic_slice_in_dim(mix_t, core_index * mix_half, mix_half, axis=1)
    held = skew(held)
    for mask in XORS[:-1]:
        held = join(held, across(held, "y", mask))
    brought = across(held, "y", XORS[-1])

    rows = latent_queries.shape[0] // 2
    asked = lax.dynamic_slice_in_dim(latent_queries, core_index * rows, rows, axis=0)
    asked = jnp.stack([asked[:, g * width : (g + 1) * width] for g in range(groups)], axis=0)
    asked = jnp.broadcast_to(asked[:, None], (groups, members, rows, width))
    asked = asked.reshape(groups * members, rows, width)
    asked = all_to_all(asked, ("x", "z"))
    asked = asked.reshape(groups * members * rows, width)
    asked_other = partner(asked)

    far_low = above[:half]
    far_low = shift(far_low, "x", -1)
    far_high = below[half:]
    far_high = shift(far_high, "x", 1)
    latents = groups * members * rows * 2
    parts = attend(
        jnp.stack([core_index, place]).astype(jnp.int32),
        asked,
        asked_other,
        kv_weight,
        (mine, above, below, far_low, far_high),
        groups,
        members,
        latents // 2,
    )
    parts = all_to_all(parts, "z")

    queries = []
    for k in range(groups):
        to = (place + k) % groups
        sent = lax.dynamic_slice_in_dim(output_queries[0], to * width, width, axis=1)
        queries.append(shift(sent, "x", k) if k else sent)
    mix_mine = order(scalar(lax.axis_index("z") ^ lax.axis_index("y")), held, brought)
    mix_other = partner(mix_mine)

    window = all_to_all(combine(parts, groups), "x")
    own, one, two = products(core, window, mix_gain[None], mix_mine, mix_other)
    one = from_behind(one, FRAME, 1)
    two = from_behind(two, FRAME, 2)
    mixed = finish(own, one, two, members, 3 * latent_width)
    mixed = all_to_all(mixed, "z").reshape(latents, width)

    decoded = decode(scalar(place), mixed, tuple(queries))
    decoded = all_to_all(decoded, "x")
    return jnp.concatenate([decoded[g] for g in range(groups)], axis=1)[None]


def solution(mesh):
    grid = Mesh(mesh.devices.reshape(8, 2, 4, 8), ("y", "core", "x", "z"))
    tok = ("x", "z")
    return jax.shard_map(
        local,
        mesh=grid,
        in_specs=(P(FRAME, tok, None), P(), P(tok, None), P(), P(None, tok), P(FRAME, tok, None)),
        out_specs=P(FRAME, tok, None),
        check_vma=False,
    )
```

```python
import math

import jax
import jax.numpy as jnp
from jax import lax
from jax.experimental import pallas as pl
from jax.experimental.pallas import tpu as pltpu
from jax.sharding import Mesh
from jax.sharding import PartitionSpec as P


HEADS = 8
HEAD_DIM = 128
EXP2_SCALE = math.log2(math.e) / math.sqrt(HEAD_DIM)
FRAME = ("y", "core")
EXTRA = 8
CHUNK = 768
TAIL = 8
XORS = (4, 2, 1)
MASKS = (0, 4, 2, 6, 1, 5, 3, 7)
VMEM_BYTES = 20 * 1024 * 1024
INTERPRET = False


def shift(block, axis, distance):
    size = lax.axis_size(axis)
    return lax.ppermute(block, axis, [(i, (i + distance) % size) for i in range(size)])


def from_behind(block, axis, distance):
    devices = range(lax.axis_size(axis))
    route = [(i - distance, i) for i in devices if i - distance in devices]
    return lax.ppermute(block, axis, route)


def across(block, axis, mask):
    return lax.ppermute(block, axis, [(i, i ^ mask) for i in range(lax.axis_size(axis))])


def partner(block):
    return lax.ppermute(block, "core", [(0, 1), (1, 0)])


def dot_nt(a, b):
    return lax.dot_general(a, b, (((1,), (1,)), ((), ())), preferred_element_type=jnp.float32)


def whole_spec(block):
    return pl.BlockSpec(block.shape, lambda i: (0,) * len(block.shape))


def head_cols(h):
    return slice(h * HEAD_DIM, (h + 1) * HEAD_DIM)


def project_inputs(in_refs, w_refs, kv_ref):
    low = 0
    for in_ref in in_refs:
        rows = in_ref.shape[0]
        left = 0
        for w_ref in w_refs:
            width = w_ref.shape[1]
            kv_ref[low : low + rows, left : left + width] = jnp.dot(
                in_ref[...], w_ref[...], preferred_element_type=jnp.float32
            ).astype(jnp.bfloat16)
            left += width
        low += rows


def pick_queries(spot_ref, mine_ref, other_ref, tile_ref):
    step = pl.program_id(0)
    tile = tile_ref.shape[0]
    per_half = mine_ref.shape[0] // tile
    start = pl.multiple_of((step % per_half) * tile, tile)
    is_mine = step // per_half == spot_ref[0]

    @pl.when(is_mine)
    def _():
        tile_ref[...] = mine_ref[pl.ds(start, tile), :]

    @pl.when(jnp.logical_not(is_mine))
    def _():
        tile_ref[...] = other_ref[pl.ds(start, tile), :]


def lanes(values, shape):
    lane = lax.broadcasted_iota(jnp.int32, shape, 1)
    result = jnp.broadcast_to(values[-1], shape)
    for k in range(len(values) - 2, -1, -1):
        result = jnp.where(lane == k, values[k], result)
    return result


def attend_body(spot_ref, mine_ref, other_ref, key_ref, value_ref, *refs):
    in_refs, (out_ref, kv_ref, q_ref) = refs[:-3], refs[-3:]
    width = mine_ref.shape[1]

    @pl.when(pl.program_id(0) == 0)
    def _():
        project_inputs(in_refs, (key_ref, value_ref), kv_ref)

    pick_queries(spot_ref, mine_ref, other_ref, q_ref)
    tile = q_ref.shape[0]
    blocks = out_ref.shape[0]
    rows = tile // blocks
    heads = range(width // HEAD_DIM)
    states = [None for _ in heads]
    count = kv_ref.shape[0]
    chunk = CHUNK if count % CHUNK == 0 else count
    for low in range(0, count, chunk):
        span = slice(low, low + chunk)
        for h in heads:
            scores = dot_nt(q_ref[:, head_cols(h)], kv_ref[span, head_cols(h)])
            peak = jnp.max(scores, axis=1, keepdims=True)
            if states[h] is not None:
                peak = jnp.maximum(peak, states[h][0])
            weights = jnp.exp2((scores - peak) * EXP2_SCALE)
            den = jnp.sum(weights, axis=1, keepdims=True)
            values = kv_ref[span, width + h * HEAD_DIM : width + (h + 1) * HEAD_DIM]
            num = jnp.dot(weights.astype(jnp.bfloat16), values, preferred_element_type=jnp.float32)
            if states[h] is not None:
                rescale = jnp.exp2((states[h][0] - peak) * EXP2_SCALE)
                den = den + rescale * states[h][1]
                num = num + rescale * states[h][2]
            states[h] = (peak, den, num)
    for h in heads:
        cols = head_cols(h)
        peak, den, num = states[h]
        first = peak.astype(jnp.bfloat16).astype(jnp.float32)
        second = (peak - first).astype(jnp.bfloat16).astype(jnp.float32)
        packed = lanes([first, second, peak - first - second, den], (tile, HEAD_DIM)).T
        for b in range(blocks):
            span = slice(b * rows, (b + 1) * rows)
            out_ref[b, :rows, cols] = num[span].astype(jnp.bfloat16)
            out_ref[b, rows:, cols] = packed[:EXTRA, span].astype(jnp.bfloat16)


def attend(spot, mine, other, kv_weight, inputs, groups, blocks, tile):
    half, width = mine.shape
    latents = 2 * half
    rows = latents // blocks

    def still(block):
        return pl.BlockSpec(block.shape, lambda i, spot_ref: (0, 0))

    if not INTERPRET:
        kv_weight = pltpu.with_memory_space_constraint(kv_weight, pltpu.HBM)
    depth = kv_weight.shape[0]
    keys = pl.BlockSpec((depth, width), lambda i, spot_ref: (0, spot_ref[1]))
    values = pl.BlockSpec((depth, width), lambda i, spot_ref: (0, groups + spot_ref[1]))
    return pl.pallas_call(
        attend_body,
        grid_spec=pltpu.PrefetchScalarGridSpec(
            num_scalar_prefetch=1,
            grid=(latents // tile,),
            in_specs=[still(mine), still(other), keys, values] + [still(b) for b in inputs],
            out_specs=pl.BlockSpec(
                (tile // rows, rows + EXTRA, width), lambda i, spot_ref: (i, 0, 0)
            ),
            scratch_shapes=[
                pltpu.VMEM((sum(b.shape[0] for b in inputs), 2 * width), jnp.bfloat16),
                pltpu.VMEM((tile, width), jnp.bfloat16),
            ],
        ),
        out_shape=jax.ShapeDtypeStruct((blocks, rows + EXTRA, width), jnp.bfloat16),
        compiler_params=pltpu.CompilerParams(vmem_limit_bytes=VMEM_BYTES),
        interpret=INTERPRET,
        name="attend",
    )(spot, mine, other, kv_weight, kv_weight, *inputs)


def order_body(place_ref, first_ref, second_ref, out_ref):
    rows = out_ref.shape[0] // len(MASKS)
    half = len(MASKS) // 2
    for j, mask in enumerate(MASKS):
        part_ref = (first_ref, second_ref)[j // half]
        low = (j % half) * rows
        at = pl.multiple_of((place_ref[0] ^ mask) * rows, rows)
        out_ref[pl.ds(at, rows), :] = part_ref[low : low + rows, :]


def order(place, first, second):
    shape = (2 * first.shape[0], first.shape[1])
    return pl.pallas_call(
        order_body,
        grid=(1,),
        in_specs=[pl.BlockSpec(memory_space=pltpu.SMEM), whole_spec(first), whole_spec(second)],
        out_specs=pl.BlockSpec(shape, lambda i: (0, 0)),
        out_shape=jax.ShapeDtypeStruct(shape, first.dtype),
        compiler_params=pltpu.CompilerParams(vmem_limit_bytes=VMEM_BYTES // 2),
        interpret=INTERPRET,
        name="order",
    )(place, first, second)


def combine_body(part_ref, out_ref):
    blocks, height, width = part_ref.shape
    rows = height - EXTRA
    groups = out_ref.shape[0]
    peaks = []
    dens = []
    for b in range(blocks):
        extra = part_ref[b, rows:, :].astype(jnp.float32)
        peaks.append(extra[0:1] + extra[1:2] + extra[2:3])
        dens.append(extra[3:4])
    top = peaks[0]
    for peak in peaks[1:]:
        top = jnp.maximum(top, peak)
    scales = [jnp.exp2((peak - top) * EXP2_SCALE) for peak in peaks]
    den = scales[0] * dens[0]
    for scale, part in zip(scales[1:], dens[1:]):
        den = den + scale * part
    pad = jnp.zeros((HEAD_DIM - blocks - 1, width), jnp.float32)
    table = jnp.concatenate(scales + [den, pad], axis=0)
    for h in range(width // HEAD_DIM):
        cols = head_cols(h)
        turned = table[:, cols].T
        total = jnp.zeros((rows, HEAD_DIM), jnp.float32)
        for b in range(blocks):
            total = total + part_ref[b, :rows, cols].astype(jnp.float32) * turned[:, b : b + 1]
        latents = (total / turned[:, blocks : blocks + 1]).astype(jnp.bfloat16)
        for g in range(groups):
            out_ref[g, :, cols] = latents


def combine(parts, groups):
    _, height, width = parts.shape
    rows = height - EXTRA
    return pl.pallas_call(
        combine_body,
        grid=(1,),
        in_specs=[whole_spec(parts)],
        out_specs=pl.BlockSpec((groups, rows, width), lambda i: (0, 0, 0)),
        out_shape=jax.ShapeDtypeStruct((groups, rows, width), jnp.bfloat16),
        compiler_params=pltpu.CompilerParams(vmem_limit_bytes=VMEM_BYTES // 2),
        interpret=INTERPRET,
        name="combine",
    )(parts)


def turn(column):
    return jnp.broadcast_to(column, (column.shape[0], HEAD_DIM)).T


def products_body(core_ref, rows_ref, gain_ref, mine_ref, other_ref, own_ref, one_ref, two_ref):
    groups, _, width = rows_ref.shape
    full = groups * width
    half = mine_ref.shape[1]
    count = own_ref.shape[0] - TAIL
    squares = jnp.zeros((count, 1), jnp.float32)
    for g in range(groups):
        block = rows_ref[g].astype(jnp.float32)
        squares = squares + jnp.sum(block * block, axis=1, keepdims=True)
    tail = turn(squares)[:TAIL]
    outs = (own_ref, one_ref, two_ref)
    for out_ref in outs:
        for h in range(width // HEAD_DIM):
            out_ref[count:, head_cols(h)] = tail

    def multiply(halves):
        for t, out_ref in enumerate(outs):
            total = jnp.zeros((count, width), jnp.float32)
            for g in range(groups):
                low = t * full + g * width
                block = rows_ref[g].astype(jnp.float32) * gain_ref[:, low : low + width]
                part_ref = halves[low // half]
                at = low % half
                total = total + dot_nt(block.astype(jnp.bfloat16), part_ref[:, at : at + width])
            out_ref[:count, :] = total

    @pl.when(core_ref[0] == 0)
    def _():
        multiply((mine_ref, other_ref))

    @pl.when(core_ref[0] != 0)
    def _():
        multiply((other_ref, mine_ref))


def products(core, window, gain, mine, other):
    _, count, width = window.shape
    return pl.pallas_call(
        products_body,
        grid=(1,),
        in_specs=[
            pl.BlockSpec(memory_space=pltpu.SMEM),
        ]
        + [whole_spec(block) for block in (window, gain, mine, other)],
        out_specs=(pl.BlockSpec((count + TAIL, width), lambda i: (0, 0)),) * 3,
        out_shape=(jax.ShapeDtypeStruct((count + TAIL, width), jnp.float32),) * 3,
        compiler_params=pltpu.CompilerParams(vmem_limit_bytes=VMEM_BYTES),
        interpret=INTERPRET,
        name="products",
    )(core, window, gain, mine, other)


def finish_body(own_ref, one_ref, two_ref, out_ref, *, features):
    members, count, width = out_ref.shape
    squares = own_ref[count:, :] + one_ref[count:, :] + two_ref[count:, :]
    inverse = lax.rsqrt(squares / features + 1e-06)
    for h in range(width // HEAD_DIM):
        cols = head_cols(h)
        pad = jnp.zeros((HEAD_DIM - TAIL, HEAD_DIM), jnp.float32)
        column = jnp.concatenate([inverse[:, cols], pad], axis=0).T[:, :1]
        product = own_ref[:count, cols] + one_ref[:count, cols] + two_ref[:count, cols]
        value = product * column
        mixed = (0.5 * value * (1.0 + lax.erf(value * math.sqrt(0.5)))).astype(jnp.bfloat16)
        for m in range(members):
            out_ref[m, :, cols] = mixed


def finish(own, one, two, members, features):
    height, width = own.shape
    return pl.pallas_call(
        lambda *refs: finish_body(*refs, features=features),
        grid=(1,),
        in_specs=[whole_spec(own), whole_spec(one), whole_spec(two)],
        out_specs=pl.BlockSpec((members, height - TAIL, width), lambda i: (0, 0, 0)),
        out_shape=jax.ShapeDtypeStruct((members, height - TAIL, width), jnp.bfloat16),
        compiler_params=pltpu.CompilerParams(vmem_limit_bytes=VMEM_BYTES // 2),
        interpret=INTERPRET,
        name="finish",
    )(own, one, two)


def decode_body(place_ref, mixed_ref, *refs):
    query_refs, out_ref = refs[:-1], refs[-1]
    groups, rows, width = out_ref.shape
    pair = 2
    blocks = [(ref, low) for ref in query_refs for low in range(0, ref.shape[0], rows)]
    for k in range(0, groups, pair):
        for h in range(width // HEAD_DIM):
            cols = head_cols(h)
            queries = [ref[low : low + rows, cols] for ref, low in blocks[k : k + pair]]
            queries = jnp.concatenate(queries, axis=0)
            scores = dot_nt(queries, mixed_ref[:, cols])
            peak = jnp.max(scores, axis=1, keepdims=True)
            weights = jnp.exp2((scores - peak) * EXP2_SCALE)
            den = jnp.sum(weights, axis=1, keepdims=True)
            result = jnp.dot(
                weights.astype(jnp.bfloat16), mixed_ref[:, cols], preferred_element_type=jnp.float32
            )
            result = result / den
            for p in range(pair):
                at = (place_ref[0] + groups - k - p) % groups
                out_ref[at, :, cols] = result[p * rows : (p + 1) * rows]


def decode(place, mixed, queries):
    rows, width = queries[0].shape
    shape = (sum(block.shape[0] for block in queries) // rows, rows, width)
    return pl.pallas_call(
        decode_body,
        grid=(1,),
        in_specs=[pl.BlockSpec(memory_space=pltpu.SMEM)]
        + [whole_spec(block) for block in (mixed,) + queries],
        out_specs=pl.BlockSpec(shape, lambda i: (0, 0, 0)),
        out_shape=jax.ShapeDtypeStruct(shape, jnp.float32),
        compiler_params=pltpu.CompilerParams(vmem_limit_bytes=VMEM_BYTES),
        interpret=INTERPRET,
        name="decode",
    )(place, mixed, *queries)


def scalar(index):
    return index.reshape(1).astype(jnp.int32)


def join(*blocks):
    return jnp.concatenate(blocks, axis=0)


def all_to_all(block, axis):
    return lax.all_to_all(block, axis, 0, 0, tiled=True)


def local(inputs, kv_weight, latent_queries, mix_gain, mix_weight, output_queries):
    groups = lax.axis_size("x")
    members = lax.axis_size("z")
    place = lax.axis_index("x")
    core_index = lax.axis_index("core")
    core = scalar(core_index)
    latent_width = HEADS * HEAD_DIM
    width = latent_width // groups

    mine = inputs[0]
    half = mine.shape[0] // 2
    above = shift(mine, "x", -1)
    below = shift(mine, "x", 1)

    mix_t = mix_weight.T
    mix_half = mix_t.shape[1] // 2
    held = lax.dynamic_slice_in_dim(mix_t, core_index * mix_half, mix_half, axis=1)
    for mask in XORS[:-1]:
        held = join(held, across(held, "z", mask))
    brought = across(held, "z", XORS[-1])

    rows = latent_queries.shape[0] // 2
    asked = lax.dynamic_slice_in_dim(latent_queries, core_index * rows, rows, axis=0)
    asked = jnp.stack([asked[:, g * width : (g + 1) * width] for g in range(groups)], axis=0)
    asked = jnp.broadcast_to(asked[:, None], (groups, members, rows, width))
    asked = asked.reshape(groups * members, rows, width)
    asked = all_to_all(asked, ("x", "z"))
    asked = asked.reshape(groups * members * rows, width)
    asked_other = partner(asked)

    far_low = above[:half]
    far_low = shift(far_low, "x", -1)
    far_high = below[half:]
    far_high = shift(far_high, "x", 1)
    latents = groups * members * rows * 2
    parts = attend(
        jnp.stack([core_index, place]).astype(jnp.int32),
        asked,
        asked_other,
        kv_weight,
        (mine, above, below, far_low, far_high),
        groups,
        members,
        latents // 2,
    )
    parts = all_to_all(parts, "z")

    queries = []
    for k in range(groups):
        to = (place + k) % groups
        sent = lax.dynamic_slice_in_dim(output_queries[0], to * width, width, axis=1)
        queries.append(shift(sent, "x", k) if k else sent)
    early = lax.optimization_barrier(join(*queries[1:3]))
    queries = [queries[0], early] + queries[3:]
    mix_mine = order(scalar(lax.axis_index("z")), held, brought)
    mix_other = partner(mix_mine)

    window = all_to_all(combine(parts, groups), "x")
    own, one, two = products(core, window, mix_gain[None], mix_mine, mix_other)
    one = from_behind(one, FRAME, 1)
    two = from_behind(two, FRAME, 2)
    mixed = finish(own, one, two, members, 3 * latent_width)
    mixed = all_to_all(mixed, "z").reshape(latents, width)

    decoded = decode(scalar(place), mixed, tuple(queries))
    decoded = all_to_all(decoded, "x")
    return jnp.concatenate([decoded[g] for g in range(groups)], axis=1)[None]


def solution(mesh):
    grid = Mesh(mesh.devices.reshape(8, 2, 4, 8), ("y", "core", "x", "z"))
    tok = ("x", "z")
    return jax.shard_map(
        local,
        mesh=grid,
        in_specs=(P(FRAME, tok, None), P(), P(tok, None), P(), P(None, tok), P(FRAME, tok, None)),
        out_specs=P(FRAME, tok, None),
        check_vma=False,
    )
```
